256 devices in a mesh: seq: 32 (over z, x), head: 8 (over y, core).
Axes of the slice: x: 4, y: 4, z: 8, core: 2. Of those that a mesh axis runs over, the one named last changes fastest.
Arguments:
- query: bfloat16 [131072, 1024], P('seq', 'head'), may hold values from -6 to 6
- key: bfloat16 [131072, 1024], P('seq', 'head'), may hold values from -6 to 6
- value: bfloat16 [131072, 1024], P('seq', 'head'), may hold values from -6 to 6
- grad_out: bfloat16 [131072, 1024], P('seq', 'head'), may hold values from -6 to 6
- random_blocks: int32 [1024, 2], P('seq'), may hold values from 0 to 1023, as said below
Outputs:
- attended: bfloat16 [131072, 1024], P('seq', 'head')
- grad_query: bfloat16 [131072, 1024], P('seq', 'head')
- grad_key: bfloat16 [131072, 1024], P('seq', 'head')
- grad_value: bfloat16 [131072, 1024], P('seq', 'head')
The draws below stay inside these ranges and needn't reach their ends.
Inputs may be any that keep to these rules, and one draw needn't show every extreme that they name: `random_blocks`: entry [j, t] names the t-th random key block of query block j. Among the 64 entries of the query blocks of one seq shard, at most 3 name blocks of any one shard (blocks s * 32 to (s + 1) * 32 - 1), and in every shard's entries some shard is named exactly 3 times.
All inputs are finite; a program needn't handle non-finite values.
Results may differ from the reference program's by a relative error of at most 0.019.
Values may be sent and summed in bfloat16 or wider, within the bound.
No kernel may reach another device: no remote copies, remote signals or barrier semaphores. Data moves between devices by JAX's collectives and lax.ppermute only.
A program may use at most 192 MiB of HBM per device.

```python
import jax
import jax.numpy as jnp
from jax import lax

HEADS = 16
HEAD_DIM = 64
BLOCK = 128
NB_DEV = 32
DMODEL = 1024
NBLK = 1024
SEQ_LEN = 131072
CAP = 3
N_SEQ = 32


def rising(top):
    place = jnp.arange(SEQ_LEN).astype(jnp.float32) / SEQ_LEN
    return (0.6 + (top - 0.6) * place)[:, None]


def first_rows():
    return (jnp.arange(SEQ_LEN) < BLOCK)[:, None]


def draw_query(key, part):
    filled = jax.random.normal(jax.random.fold_in(key, 1), (SEQ_LEN, DMODEL))
    filled = jnp.where(first_rows(), 2.0 * filled, filled)
    filled = jnp.clip(filled, -6.0, 6.0)
    return filled.astype(jnp.bfloat16)


def draw_key(key, part):
    filled = jax.random.normal(jax.random.fold_in(key, 2), (SEQ_LEN, DMODEL)) * rising(1.2)
    filled = jnp.clip(filled, -6.0, 6.0)
    return filled.astype(jnp.bfloat16)


def draw_random_blocks(key, part):

    def shard_rows(shard_id):
        shard_key = jax.random.fold_in(jax.random.fold_in(key, 5), shard_id)
        first_key, second_key, third_key = jax.random.split(shard_key, 3)
        slot_ids = jax.random.permutation(first_key, N_SEQ * CAP)
        owners = (slot_ids // CAP).astype(jnp.int32)
        busiest = owners[0]
        ordering = jnp.argsort((owners == busiest).astype(jnp.int32), stable=True)
        others = owners[ordering][:2 * NB_DEV - CAP]
        picked = jnp.concatenate([jnp.full((CAP,), busiest, jnp.int32), others])
        picked = jax.random.permutation(second_key, picked)
        inner = jax.random.randint(third_key, (2 * NB_DEV,), 0, NB_DEV)
        return (picked * NB_DEV + inner).astype(jnp.int32)
    table = jax.vmap(shard_rows)(jnp.arange(N_SEQ, dtype=jnp.int32))
    return table.reshape(NBLK, 2)


def block_levels(stream_key, dims, pieces, smallest, high):
    factor_of, own = 1.0, jax.random.fold_in(stream_key, 6)
    for axis_at, blocks in pieces:
        heights = jnp.exp(jax.random.uniform(jax.random.fold_in(own, axis_at), (blocks,), jnp.float32, smallest / len(pieces), high / len(pieces)))
        factor_of = factor_of * jnp.repeat(heights, dims[axis_at] // blocks).reshape([-1 if axis == axis_at else 1 for axis in range(len(dims))])
    return factor_of


def gaussian(own_key, extent, spread, limit, shards=(), held_as=jnp.bfloat16):
    entries = jax.random.normal(own_key, extent, jnp.float32) * spread
    if len(shards) > 0:
        entries = block_levels(own_key, extent, shards, -0.22, 0.18) * entries
    return jnp.clip(entries, min=-limit, max=limit).astype(held_as)


def setup_inputs(seed: int = 0) -> dict:
    streams_of = jax.random.split(jax.random.key(seed), 6)
    query = draw_query(jax.random.fold_in(streams_of[5], 71), 0)
    key = draw_key(jax.random.fold_in(streams_of[5], 71), 0)
    value = gaussian(streams_of[2], (SEQ_LEN, DMODEL), 1.0, 6.0, ((0, 32), (1, 8)))
    grad_out = gaussian(streams_of[3], (SEQ_LEN, DMODEL), 1.0, 6.0, ((0, 32), (1, 8)))
    random_blocks = draw_random_blocks(jax.random.fold_in(streams_of[5], 71), 0)
    return dict(query=query, key=key, value=value, grad_out=grad_out, random_blocks=random_blocks)


def log_totals(scores):
    peak = jnp.max(scores, axis=-1)
    summed = jnp.sum(jnp.exp(scores - peak[..., None]), axis=-1)
    return peak + jnp.log(summed)


def reference(query, key, value, grad_out, random_blocks):
    score_scale = HEAD_DIM ** -0.5
    query_blocks = query.reshape(NBLK, BLOCK, HEADS, HEAD_DIM)
    key_blocks = key.reshape(NBLK, BLOCK, HEADS, HEAD_DIM)
    value_blocks = value.reshape(NBLK, BLOCK, HEADS, HEAD_DIM)
    grad_blocks = grad_out.reshape(NBLK, BLOCK, HEADS, HEAD_DIM)
    column_block = jnp.arange(6 * BLOCK, dtype=jnp.int32) // BLOCK

    def regular(carry, block_index):
        key_acc, value_acc = carry
        chosen = jnp.stack([block_index - 1, block_index, jnp.minimum(block_index + 1, NBLK - 1),
                            random_blocks[block_index, 0], random_blocks[block_index, 1],
                            jnp.zeros((), jnp.int32)]).astype(jnp.int32)
        key_tiles = key_blocks[chosen].astype(jnp.float32).reshape(6 * BLOCK, HEADS, HEAD_DIM)
        value_tiles = value_blocks[chosen].astype(jnp.float32).reshape(6 * BLOCK, HEADS, HEAD_DIM)
        query_tiles = query_blocks[block_index].astype(jnp.float32)
        grad_tiles = grad_blocks[block_index].astype(jnp.float32)
        scores = jnp.einsum("qhe,khe->hqk", query_tiles, key_tiles) * score_scale
        allowed = (column_block != 2) | (block_index + 1 < NBLK)
        scores = jnp.where(allowed[None, None, :], scores, -jnp.inf)
        totals = log_totals(scores)
        weights = jnp.exp(scores - totals[..., None])
        weights_low = lax.optimization_barrier(weights.astype(jnp.bfloat16)).astype(jnp.float32)
        attended = jnp.einsum("hqk,khe->qhe", weights_low, value_tiles).astype(jnp.bfloat16)
        row_dots = jnp.sum(grad_tiles * lax.optimization_barrier(attended).astype(jnp.float32), axis=-1).T
        grad_weights = jnp.einsum("qhe,khe->hqk", grad_tiles, value_tiles)
        grad_scores = weights * (grad_weights - row_dots[..., None])
        grad_scores = lax.optimization_barrier(grad_scores.astype(jnp.bfloat16)).astype(jnp.float32)
        grad_rows = (jnp.einsum("hqk,khe->qhe", grad_scores, key_tiles) * score_scale).astype(jnp.bfloat16)
        key_terms = jnp.einsum("hqk,qhe->khe", grad_scores, query_tiles) * score_scale
        value_terms = jnp.einsum("hqk,qhe->khe", weights_low, grad_tiles)
        key_acc = key_acc.at[chosen].add(key_terms.reshape(6, BLOCK, HEADS, HEAD_DIM))
        value_acc = value_acc.at[chosen].add(value_terms.reshape(6, BLOCK, HEADS, HEAD_DIM))
        return (key_acc, value_acc), (attended, grad_rows)

    empty = jnp.zeros((NBLK, BLOCK, HEADS, HEAD_DIM), jnp.float32)
    (key_acc, value_acc), (attended_rest, grad_rest) = lax.scan(
        regular, (empty, empty), jnp.arange(1, NBLK, dtype=jnp.int32))

    def global_head(packed):
        head_query, head_keys, head_values, head_grad = packed
        query_tiles = head_query.astype(jnp.float32)
        key_tiles = head_keys.astype(jnp.float32)
        value_tiles = head_values.astype(jnp.float32)
        grad_tiles = head_grad.astype(jnp.float32)
        scores = jnp.einsum("qe,ke->qk", query_tiles, key_tiles) * score_scale
        totals = log_totals(scores)
        weights = jnp.exp(scores - totals[..., None])
        weights_low = lax.optimization_barrier(weights.astype(jnp.bfloat16)).astype(jnp.float32)
        attended = jnp.einsum("qk,ke->qe", weights_low, value_tiles).astype(jnp.bfloat16)
        row_dots = jnp.sum(grad_tiles * lax.optimization_barrier(attended).astype(jnp.float32), axis=-1)
        grad_weights = jnp.einsum("qe,ke->qk", grad_tiles, value_tiles)
        grad_scores = weights * (grad_weights - row_dots[:, None])
        grad_scores = lax.optimization_barrier(grad_scores.astype(jnp.bfloat16)).astype(jnp.float32)
        grad_rows = (jnp.einsum("qk,ke->qe", grad_scores, key_tiles) * score_scale).astype(jnp.bfloat16)
        key_terms = jnp.einsum("qk,qe->ke", grad_scores, query_tiles) * score_scale
        value_terms = jnp.einsum("qk,qe->ke", weights_low, grad_tiles)
        return attended, grad_rows, key_terms, value_terms

    heads_query = query[:BLOCK].reshape(BLOCK, HEADS, HEAD_DIM).transpose(1, 0, 2)
    heads_grad = grad_out[:BLOCK].reshape(BLOCK, HEADS, HEAD_DIM).transpose(1, 0, 2)
    heads_keys = key.reshape(SEQ_LEN, HEADS, HEAD_DIM).transpose(1, 0, 2)
    heads_values = value.reshape(SEQ_LEN, HEADS, HEAD_DIM).transpose(1, 0, 2)
    first_out, first_grad, far_keys, far_values = lax.map(
        global_head, (heads_query, heads_keys, heads_values, heads_grad))
    first_out = first_out.transpose(1, 0, 2).reshape(BLOCK, DMODEL)
    first_grad = first_grad.transpose(1, 0, 2).reshape(BLOCK, DMODEL)
    key_total = key_acc + far_keys.transpose(1, 0, 2).reshape(NBLK, BLOCK, HEADS, HEAD_DIM)
    value_total = value_acc + far_values.transpose(1, 0, 2).reshape(NBLK, BLOCK, HEADS, HEAD_DIM)
    attended = jnp.concatenate([first_out, attended_rest.reshape(SEQ_LEN - BLOCK, DMODEL)], axis=0)
    grad_query = jnp.concatenate([first_grad, grad_rest.reshape(SEQ_LEN - BLOCK, DMODEL)], axis=0)
    grad_key = key_total.reshape(SEQ_LEN, DMODEL).astype(jnp.bfloat16)
    grad_value = value_total.reshape(SEQ_LEN, DMODEL).astype(jnp.bfloat16)
    return (attended, grad_query, grad_key, grad_value)
```

```python
import functools
import math

import jax
import jax.numpy as jnp
from jax import lax
from jax.experimental import pallas as pl
from jax.experimental.pallas import tpu as pltpu
from jax.sharding import PartitionSpec as P

HEAD_DIM = 64
BLOCK = 128
CAP = 3
LOG2E = math.log2(math.e)
SCALE = HEAD_DIM**-0.5
F32 = jnp.float32
BF16 = jnp.bfloat16
VMEM_LIMIT = 52 * 1024 * 1024

in_vmem = pl.BlockSpec(memory_space=pltpu.VMEM)
in_smem = pl.BlockSpec(memory_space=pltpu.SMEM)


def params():
    return pltpu.CompilerParams(vmem_limit_bytes=VMEM_LIMIT)


def dot(a, b, a_dim, b_dim):
    return lax.dot_general(a, b, (((a_dim,), (b_dim,)), ((), ())), preferred_element_type=F32)


def low_lanes(shape):
    return lax.broadcasted_iota(jnp.int32, shape, len(shape) - 1) < HEAD_DIM


def join(a, b):
    a, b = a.astype(F32), b.astype(F32)
    low = low_lanes(a.shape)
    axis = a.ndim - 1
    first = jnp.where(low, a, pltpu.roll(b, HEAD_DIM, axis))
    second = jnp.where(low, pltpu.roll(a, HEAD_DIM, axis), b)
    return first.astype(BF16), second.astype(BF16)


def pack_kernel(q_ref, k_ref, v_ref, g_ref, qg0_ref, qg1_ref, kv0_ref, kv1_ref):
    qg0_ref[...], qg1_ref[...] = join(q_ref[...], g_ref[...])
    kv0_ref[...], kv1_ref[...] = join(k_ref[...], v_ref[...])


def ask_kernel(asked_ref, q_ref, k_ref, v_ref, g_ref, k_end_ref, v_end_ref, out_ref, up_ref, down_ref):
    extra = 4 * BLOCK // out_ref.shape[0]
    raw = jnp.concatenate([q_ref[...], k_ref[...], v_ref[...], g_ref[...]], axis=0)
    out_ref[:, :extra] = raw.reshape(out_ref.shape[0], extra, BLOCK)
    out_ref[:, extra:] = asked_ref[...]
    up_ref[0], up_ref[1] = k_end_ref[...], v_end_ref[...]
    down_ref[0], down_ref[1] = k_ref[...], v_ref[...]


def gather0_kernel(wanted_ref, kv_ref, piece_ref, out_ref):
    def copy(d, _):
        out_ref[d, :BLOCK] = kv_ref[wanted_ref[CAP * d]]
        out_ref[d, BLOCK:] = piece_ref[...]
        return 0

    lax.fori_loop(0, out_ref.shape[0], copy, 0, unroll=2)


def gather0_rest_kernel(wanted_ref, kv_ref, out_ref):
    def copy(d, _):
        out_ref[d, :BLOCK] = kv_ref[wanted_ref[CAP * d + 1]]
        out_ref[d, BLOCK:] = kv_ref[wanted_ref[CAP * d + 2]]
        return 0

    lax.fori_loop(0, out_ref.shape[0], copy, 0, unroll=2)


def gather1_kernel(wanted_ref, kv_ref, piece_ref, out_ref):
    def copy(d, _):
        for r in range(CAP):
            out_ref[d, r * BLOCK : (r + 1) * BLOCK] = kv_ref[wanted_ref[CAP * d + r]]
        out_ref[d, CAP * BLOCK :] = piece_ref[...]
        return 0

    lax.fori_loop(0, out_ref.shape[0], copy, 0, unroll=2)


def query_pair(qg):
    low = low_lanes(qg.shape)
    return jnp.concatenate(
        [jnp.where(low, qg * SCALE, 0.0).astype(BF16), jnp.where(low, 0.0, qg).astype(BF16)], axis=0
    )


def main0_kernel(
    slot_ref, edge_ref, qg_ref, kv_ref, low_ref, high_ref, one_ref, two_ref, raw_ref,
    od_ref, back_ref, acc_ref, side_ref, col_ref, pad_ref, far_ref, ret_ref,
):
    def spread(d, _):
        far_ref[CAP * d] = one_ref[d, :BLOCK]
        far_ref[CAP * d + 1] = two_ref[d, :BLOCK]
        far_ref[CAP * d + 2] = two_ref[d, BLOCK:]
        return 0

    lax.fori_loop(0, one_ref.shape[0], spread, 0)
    attend(
        0, slot_ref, edge_ref, qg_ref, kv_ref, low_ref, high_ref, far_ref, raw_ref,
        od_ref, ret_ref, acc_ref, side_ref, col_ref, pad_ref,
    )

    def collect(d, _):
        for r in range(CAP):
            back_ref[d, r * BLOCK : (r + 1) * BLOCK] = ret_ref[CAP * d + r]
        return 0

    lax.fori_loop(0, one_ref.shape[0], collect, 0)


def main1_kernel(
    slot_ref, edge_ref, qg_ref, kv_ref, low_ref, high_ref, three_ref, raw_ref, row_ref, col0_ref,
    od_ref, two_ref, one_ref, acc_ref, side_ref, pad_ref, far_ref, ret_ref, col_ref,
):
    shards, extra = one_ref.shape[0], one_ref.shape[1] - BLOCK

    def spread(d, _):
        for r in range(CAP):
            far_ref[CAP * d + r] = three_ref[d, r * BLOCK : (r + 1) * BLOCK]
        return 0

    lax.fori_loop(0, shards, spread, 0)
    attend(
        1, slot_ref, edge_ref, qg_ref, kv_ref, low_ref, high_ref, far_ref, raw_ref,
        od_ref, ret_ref, acc_ref, side_ref, col_ref, pad_ref,
    )

    def collect(d, _):
        two_ref[d, :BLOCK] = ret_ref[CAP * d]
        two_ref[d, BLOCK : 2 * BLOCK] = ret_ref[CAP * d + 1]
        one_ref[d, :BLOCK] = ret_ref[CAP * d + 2]
        return 0

    lax.fori_loop(0, shards, collect, 0)
    parts = [row_ref[0], row_ref[1], col0_ref[...], col_ref[...]]
    parts = jnp.concatenate([x.astype(BF16) for x in parts], axis=0)
    two_ref[:, 2 * BLOCK :] = parts.reshape(shards, extra, BLOCK)
    one_ref[:, BLOCK:] = jnp.zeros((shards, extra, BLOCK), BF16)


def attend(
    head, slot_ref, edge_ref, qg_ref, kv_ref, low_ref, high_ref, far_ref, raw_ref,
    od_ref, ret_ref, acc_ref, side_ref, col_ref, pad_ref,
):
    blocks = qg_ref.shape[0]
    is_first, is_last = edge_ref[0], edge_ref[1]
    first = join(raw_ref[BLOCK : 2 * BLOCK], raw_ref[2 * BLOCK : 3 * BLOCK])[head]
    pad_ref[0] = join(low_ref[0], low_ref[1])[head]
    pad_ref[blocks + 1] = join(high_ref[0], high_ref[1])[head]
    pad_ref[1 : blocks + 1] = kv_ref[...]
    acc_ref[...] = jnp.zeros_like(acc_ref)
    ret_ref[...] = jnp.zeros_like(ret_ref)
    col_ref[...] = jnp.zeros_like(col_ref)

    def step(j, _):
        slot0, slot1 = slot_ref[2 * j], slot_ref[2 * j + 1]
        keep = 1.0 - ((j == 0) & (is_first == 1)).astype(F32)
        qg = qg_ref[j].astype(F32) * keep
        pair = query_pair(qg)
        window = pad_ref[pl.ds(j, 3)].reshape(3 * BLOCK, BLOCK)
        kv = jnp.concatenate([window, far_ref[slot0], far_ref[slot1], first], axis=0)
        both = dot(kv, pair, 1, 1)
        scores, gw = both[:, :BLOCK], both[:, BLOCK:]
        drop = (j == blocks - 1) & (is_last == 1)
        bias = jnp.where(drop, -jnp.inf, 0.0).astype(F32)
        scores = jnp.concatenate(
            [scores[: 2 * BLOCK], scores[2 * BLOCK : 3 * BLOCK] + bias, scores[3 * BLOCK :]], axis=0
        )
        peak = jnp.max(scores, axis=0, keepdims=True)
        expo = jnp.exp2((scores - peak) * LOG2E)
        weights = expo * (1.0 / jnp.sum(expo, axis=0, keepdims=True))
        wlow = weights.astype(BF16)
        kvt = kv.T
        out_t = dot(kvt, wlow, 1, 0)
        rounded = out_t.astype(BF16).astype(F32)
        row_dot = jnp.sum((rounded * qg.T)[HEAD_DIM:], axis=0, keepdims=True)
        ds = (weights * (gw - row_dot)).astype(BF16)
        dq_t = dot(kvt, ds, 1, 0)
        od_t = jnp.concatenate([dq_t[:HEAD_DIM] * SCALE, out_t[HEAD_DIM:]], axis=0)
        od_ref[j] = od_t.T.astype(BF16)
        terms = dot(jnp.concatenate([ds, wlow], axis=1), pair, 1, 0)
        acc_ref[pl.ds(j, 3)] += terms[: 3 * BLOCK].reshape(3, BLOCK, BLOCK)
        ret_ref[slot0] = terms[3 * BLOCK : 4 * BLOCK].astype(BF16)
        ret_ref[slot1] = terms[4 * BLOCK : 5 * BLOCK].astype(BF16)
        col_ref[...] += terms[5 * BLOCK :]
        return 0

    lax.fori_loop(0, blocks, step, 0)
    side_ref[0] = acc_ref[0].astype(BF16)
    side_ref[1] = acc_ref[blocks + 1].astype(BF16)


def raw_query(raw_ref):
    return join(raw_ref[:BLOCK], raw_ref[3 * BLOCK :])


def two_parts(x):
    high = x.astype(BF16)
    return high, (x - high.astype(F32)).astype(BF16)


def row_forward_kernel(raw_ref, kv0_ref, kv1_ref, stats_ref, peak_ref, out_ref, *, chunk):
    rows = []
    for h, kv_ref in enumerate((kv0_ref, kv1_ref)):
        qg = raw_query(raw_ref)[h].astype(F32)
        query = query_pair(qg)[:BLOCK]

        def step(c, carry, kv_ref=kv_ref, query=query):
            peak, total, out = carry
            kv = kv_ref[pl.ds(pl.multiple_of(c * chunk, chunk), chunk)]
            scores = dot(kv, query, 1, 1)
            new = jnp.maximum(peak, jnp.max(scores, axis=0, keepdims=True))
            shrink = jnp.exp2((peak - new) * LOG2E)
            expo = jnp.exp2((scores - new) * LOG2E)
            total = total * shrink + jnp.sum(expo, axis=0, keepdims=True)
            out = out * shrink + dot(kv, expo.astype(BF16), 0, 0)
            return new, total, out

        start = (
            jnp.full((1, BLOCK), -jnp.inf, F32),
            jnp.zeros((1, BLOCK), F32),
            jnp.zeros((BLOCK, BLOCK), F32),
        )
        peak, total, out = lax.fori_loop(0, kv_ref.shape[0] // chunk, step, start)
        point = peak.astype(BF16)
        shift = jnp.exp2((peak - point.astype(F32)) * LOG2E)
        out = out * shift
        row_dot = jnp.sum((out * qg.T)[HEAD_DIM:], axis=0, keepdims=True)
        rows += [point, *two_parts(total * shift), *two_parts(row_dot)]
        peak_ref[h : h + 1] = point.astype(F32)
        out_ref[h] = out
    rows = [r.astype(F32) for r in rows] + [jnp.zeros((6, BLOCK), F32)]
    stats_ref[...] = jnp.concatenate(rows, axis=0).astype(BF16)


def row_backward_kernel(
    raw_ref, kv0_ref, kv1_ref, all_ref, peak_ref, out_ref, far0_ref, far1_ref, row_ref, *, chunk
):
    stats = all_ref[...].astype(F32)
    for h, (kv_ref, far_ref) in enumerate(((kv0_ref, far0_ref), (kv1_ref, far1_ref))):
        qg = raw_query(raw_ref)[h].astype(F32)
        pair = query_pair(qg)
        row = [stats[:, 5 * h + i] for i in range(5)]
        peak = jnp.max(row[0], axis=0, keepdims=True)
        grow = jnp.exp2((row[0] - peak) * LOG2E)
        scale = 1.0 / jnp.sum((row[1] + row[2]) * grow, axis=0, keepdims=True)
        row_dot = jnp.sum((row[3] + row[4]) * grow, axis=0, keepdims=True) * scale

        def step(c, dq_t, kv_ref=kv_ref, far_ref=far_ref, pair=pair, peak=peak, scale=scale, row_dot=row_dot):
            rows = pl.ds(pl.multiple_of(c * chunk, chunk), chunk)
            kv = kv_ref[rows]
            both = dot(kv, pair, 1, 1)
            weights = jnp.exp2((both[:, :BLOCK] - peak) * LOG2E) * scale
            ds = (weights * (both[:, BLOCK:] - row_dot)).astype(BF16)
            far_ref[rows] = dot(jnp.concatenate([ds, weights.astype(BF16)], axis=1), pair, 1, 0)
            return dq_t + dot(kv, ds, 0, 0)

        dq_t = lax.fori_loop(0, kv_ref.shape[0] // chunk, step, jnp.zeros((BLOCK, BLOCK), F32))
        out_t = out_ref[h] * (jnp.exp2((peak_ref[h : h + 1] - peak) * LOG2E) * scale)
        row_ref[h] = jnp.concatenate([dq_t[:HEAD_DIM] * SCALE, out_t[HEAD_DIM:]], axis=0).T


def add_slots(tot_ref, wanted_ref, back_ref, ranks):
    def add(d, _):
        for at, r in enumerate(ranks):
            tot_ref[wanted_ref[CAP * d + r]] += back_ref[d, at * BLOCK : (at + 1) * BLOCK].astype(F32)
        return 0

    lax.fori_loop(0, back_ref.shape[0], add, 0)


def own_rows(h, tot_ref, acc_ref, far_ref, left_ref, right_ref):
    blocks = tot_ref.shape[0]
    tot_ref[...] = acc_ref[1 : blocks + 1] + far_ref[...].reshape(tot_ref.shape)
    tot_ref[blocks - 1] += right_ref[h].astype(F32)
    tot_ref[0] += left_ref[h].astype(F32)


def total0_kernel(
    wanted_ref, acc_ref, far_ref, left_ref, right_ref, three_ref, out_ref, block_ref, tot_ref
):
    own_rows(0, tot_ref, acc_ref, far_ref, left_ref, right_ref)
    add_slots(tot_ref, wanted_ref, three_ref, range(CAP))
    block_ref[...] = tot_ref[0]
    out_ref[...] = tot_ref[...].astype(BF16)


def total1_kernel(wanted_ref, acc_ref, far_ref, left_ref, right_ref, two_ref, tot_ref):
    own_rows(1, tot_ref, acc_ref, far_ref, left_ref, right_ref)
    add_slots(tot_ref, wanted_ref, two_ref, range(2))


def last_kernel(
    wanted_ref, edge_ref, part_ref, one_ref, head0_ref, block_ref, dk_ref, dv_ref, tot_ref
):
    tot_ref[...] = part_ref[...]
    add_slots(tot_ref, wanted_ref, one_ref, range(2, CAP))
    root = one_ref[:, BLOCK:].reshape(4 * BLOCK, BLOCK).astype(F32) * edge_ref[0].astype(F32)
    tot_ref[0] += root[3 * BLOCK :]

    def write(b, _):
        dk_ref[b], dv_ref[b] = join(head0_ref[b], tot_ref[b])
        return 0

    lax.fori_loop(0, tot_ref.shape[0], write, 0, unroll=2)
    dk_ref[0], dv_ref[0] = join(block_ref[...] + root[2 * BLOCK : 3 * BLOCK], tot_ref[0])


def unpack_kernel(od0_ref, od1_ref, att_ref, dq_ref):
    def write(b, _):
        dq_ref[b], att_ref[b] = join(od0_ref[b], od1_ref[b])
        return 0

    lax.fori_loop(0, od0_ref.shape[0], write, 0)


def root_kernel(edge_ref, root_ref, att_ref, dq_ref, att_out, dq_out):
    dq, att = join(root_ref[:BLOCK], root_ref[BLOCK : 2 * BLOCK])
    is_first = edge_ref[0] == 1
    att_out[...] = jnp.where(is_first, att.astype(F32), att_ref[...].astype(F32)).astype(BF16)
    dq_out[...] = jnp.where(is_first, dq.astype(F32), dq_ref[...].astype(F32)).astype(BF16)


def in_hbm(x):
    return pltpu.with_memory_space_constraint(x, pltpu.HBM)


def call(kernel, outs, operands, smem=0, scratch=(), us=2, loose=()):
    return pl.pallas_call(
        kernel,
        out_shape=[pltpu.HBM(s, d) for s, d in outs],
        in_specs=[in_smem] * smem + [in_vmem] * (len(operands) - smem),
        out_specs=[in_vmem] * len(outs),
        scratch_shapes=[pltpu.VMEM(s, d) for s, d in scratch],
        compiler_params=params(),
        cost_estimate=pl.CostEstimate(flops=us * 10**9, transcendentals=0, bytes_accessed=10**6),
    )(*(x if i < smem or i in loose else in_hbm(x) for i, x in enumerate(operands)))


def exchange(blocks):
    return lax.all_to_all(blocks, "seq", split_axis=0, concat_axis=0, tiled=True)


def after(x, done):
    return lax.optimization_barrier((x, done))


def per_device(query, key, value, grad_out, random_blocks):
    shards, here = lax.axis_size("seq"), lax.axis_index("seq")
    rows = query.shape[0]
    blocks = rows // BLOCK
    slots = shards * CAP
    extra = 4 * BLOCK // shards
    tile = (BLOCK, BLOCK)
    grid = (blocks, *tile)
    forward = [(i, i + 1) for i in range(shards - 1)]
    backward = [(i + 1, i) for i in range(shards - 1)]

    named = random_blocks.reshape(-1)
    owners, inner = named // blocks, named % blocks
    places = jnp.arange(named.shape[0])
    same = (owners[:, None] == owners[None, :]) & (places[None, :] < places[:, None])
    slot_of = owners * CAP + jnp.sum(same.astype(jnp.int32), axis=1)
    asked = jnp.sum(
        jnp.where(slot_of[None, :] == jnp.arange(slots)[:, None], inner[None, :], 0), axis=1
    ).reshape(shards, 1, CAP)
    asked = jnp.pad(asked.astype(BF16), ((0, 0), (0, 15), (0, BLOCK - CAP)))
    top = pl.BlockSpec(tile, lambda i: (0, 0))
    end = pl.BlockSpec(tile, lambda i: (blocks - 1, 0))
    query, key, value, grad_out = (in_hbm(x) for x in (query, key, value, grad_out))
    message, up, down = pl.pallas_call(
        ask_kernel,
        grid=(1,),
        out_shape=[
            pltpu.HBM((shards, extra + 16, BLOCK), BF16),
            pltpu.HBM((2, *tile), BF16),
            pltpu.HBM((2, *tile), BF16),
        ],
        in_specs=[pl.BlockSpec(asked.shape, lambda i: (0, 0, 0)), top, top, top, top, end, end],
        out_specs=[
            pl.BlockSpec((shards, extra + 16, BLOCK), lambda i: (0, 0, 0)),
            pl.BlockSpec((2, *tile), lambda i: (0, 0, 0)),
            pl.BlockSpec((2, *tile), lambda i: (0, 0, 0)),
        ],
        compiler_params=params(),
    )(asked, query, key, value, grad_out, key, value)
    low = lax.ppermute(up, "seq", forward)
    high = lax.ppermute(down, "seq", backward)
    got = exchange(message)
    wanted = got[:, extra, :CAP].astype(jnp.int32).reshape(-1)
    edge = jnp.stack([here == 0, here == shards - 1]).astype(jnp.int32)

    chunk = 512
    part = pl.BlockSpec((chunk, BLOCK), lambda i: (i, 0))
    qg0, qg1, kv0, kv1 = pl.pallas_call(
        pack_kernel,
        grid=(rows // chunk,),
        out_shape=[pltpu.HBM((rows, BLOCK), BF16)] * 4,
        in_specs=[part] * 4,
        out_specs=[part] * 4,
        compiler_params=params(),
    )(query, key, value, grad_out)
    (one0,) = call(
        gather0_kernel,
        [((shards, BLOCK + extra, BLOCK), BF16)],
        (wanted, kv0.reshape(grid), got[0, :extra]),
        smem=1,
        loose=(2,),
    )
    (two0,) = call(
        gather0_rest_kernel,
        [((shards, 2 * BLOCK, BLOCK), BF16)],
        (wanted, kv0.reshape(grid)),
        smem=1,
    )
    one0, low, high = lax.optimization_barrier((one0, low, high))
    one0 = exchange(one0)
    two0, one0 = after(two0, one0)
    two0 = exchange(two0)
    first = one0[:, BLOCK:].reshape(4 * BLOCK, BLOCK)
    stats, peak, partial = call(
        functools.partial(row_forward_kernel, chunk=chunk),
        [((16, BLOCK), BF16), ((2, BLOCK), F32), ((2, *tile), F32)],
        (first, kv0, kv1),
        us=8,
        loose=(0,),
    )
    (three1,) = call(
        gather1_kernel,
        [((shards, CAP * BLOCK + extra, BLOCK), BF16)],
        (wanted, kv1.reshape(grid), stats),
        smem=1,
        loose=(2,),
    )
    three1, two0 = after(three1, two0)
    three1 = exchange(three1)
    scratch = [((blocks + 2, *tile), BF16), ((slots, *tile), BF16), ((slots, *tile), BF16)]
    od0, back0, acc0, side0, col0 = call(
        main0_kernel,
        [
            (grid, BF16),
            ((shards, CAP * BLOCK, BLOCK), BF16),
            ((blocks + 2, *tile), F32),
            ((2, *tile), BF16),
            (tile, F32),
        ],
        (slot_of, edge, qg0.reshape(grid), kv0.reshape(grid), low, high, one0, two0, first),
        smem=2,
        loose=(4, 5, 6, 7, 8),
        scratch=scratch,
        us=38,
    )
    back0, three1 = after(back0, three1)
    back0 = exchange(back0)
    far0, far1, row_od = call(
        functools.partial(row_backward_kernel, chunk=chunk),
        [((rows, BLOCK), F32)] * 2 + [((2, *tile), F32)],
        (first, kv0, kv1, three1[:, CAP * BLOCK :], peak, partial),
        us=8,
        loose=(0, 3),
    )
    od1, two1, one1, acc1, side1 = call(
        main1_kernel,
        [
            (grid, BF16),
            ((shards, 2 * BLOCK + extra, BLOCK), BF16),
            ((shards, BLOCK + extra, BLOCK), BF16),
            ((blocks + 2, *tile), F32),
            ((2, *tile), BF16),
        ],
        (
            slot_of, edge, qg1.reshape(grid), kv1.reshape(grid), low, high, three1, first,
            row_od, col0,
        ),
        smem=2,
        loose=(4, 5, 6, 7),
        scratch=[*scratch, (tile, F32)],
        us=38,
    )
    left = lax.ppermute(jnp.stack([side0[1], side1[1]]), "seq", forward)
    right = lax.ppermute(jnp.stack([side0[0], side1[0]]), "seq", backward)
    two1, back0, left, right = lax.optimization_barrier((two1, back0, left, right))
    two1 = exchange(two1)
    total = jnp.sum(two1[:, 2 * BLOCK :].astype(F32), axis=0).astype(BF16)
    one1 = one1.at[:, BLOCK:].set(jnp.broadcast_to(total, (shards, extra, BLOCK)))
    one1 = exchange(one1)
    attended, grad_query = call(unpack_kernel, [(grid, BF16)] * 2, (od0, od1), us=4)
    whole = [(grid, F32)]
    head0, block0 = call(
        total0_kernel,
        [(grid, BF16), (tile, F32)],
        (wanted, acc0, far0, left, right, back0),
        smem=1,
        loose=(3, 4, 5),
        scratch=whole,
        us=6,
    )
    (part1,) = call(
        total1_kernel, whole, (wanted, acc1, far1, left, right, two1), smem=1, us=4, loose=(3, 4, 5)
    )
    grad_key, grad_value = call(
        last_kernel,
        [(grid, BF16)] * 2,
        (wanted, edge, part1, one1, head0, block0),
        smem=2,
        loose=(3,),
        scratch=whole,
        us=4,
    )
    attended, grad_query, grad_key, grad_value = (
        x.reshape(rows, BLOCK) for x in (attended, grad_query, grad_key, grad_value)
    )
    root = one1[:, BLOCK:].reshape(4 * BLOCK, BLOCK)
    attended, grad_query = pl.pallas_call(
        root_kernel,
        grid=(1,),
        out_shape=[pltpu.HBM((rows, BLOCK), BF16)] * 2,
        in_specs=[in_smem, pl.BlockSpec((4 * BLOCK, BLOCK), lambda i: (0, 0)), top, top],
        out_specs=[top, top],
        input_output_aliases={2: 0, 3: 1},
        compiler_params=params(),
    )(edge, root, in_hbm(attended), in_hbm(grad_query))
    return attended, grad_query, grad_key, grad_value


def solution(mesh):
    split = P("seq", "head")
    return jax.shard_map(
        per_device,
        mesh=mesh,
        in_specs=(split, split, split, split, P("seq", None)),
        out_specs=(split, split, split, split),
        check_vma=False,
    )
```

```python
import functools
import math

import jax
import jax.numpy as jnp
from jax import lax
from jax.experimental import pallas as pl
from jax.experimental.pallas import tpu as pltpu
from jax.sharding import PartitionSpec as P

HEAD_DIM = 64
BLOCK = 128
CAP = 3
LATE = BLOCK
LOG2E = math.log2(math.e)
SCALE = HEAD_DIM**-0.5
F32 = jnp.float32
BF16 = jnp.bfloat16
VMEM_LIMIT = 28 * 1024 * 1024

in_vmem = pl.BlockSpec(memory_space=pltpu.VMEM)
in_smem = pl.BlockSpec(memory_space=pltpu.SMEM)


def params():
    return pltpu.CompilerParams(vmem_limit_bytes=VMEM_LIMIT)


def dot(a, b, a_dim, b_dim):
    return lax.dot_general(a, b, (((a_dim,), (b_dim,)), ((), ())), preferred_element_type=F32)


def low_lanes(shape):
    return lax.broadcasted_iota(jnp.int32, shape, len(shape) - 1) < HEAD_DIM


def join(a, b):
    a, b = a.astype(F32), b.astype(F32)
    low = low_lanes(a.shape)
    axis = a.ndim - 1
    first = jnp.where(low, a, pltpu.roll(b, HEAD_DIM, axis))
    second = jnp.where(low, pltpu.roll(a, HEAD_DIM, axis), b)
    return first.astype(BF16), second.astype(BF16)


def pack_kernel(a_ref, b_ref, head0_ref, head1_ref):
    head0_ref[...], head1_ref[...] = join(a_ref[...], b_ref[...])


def ask_kernel(asked_ref, q_ref, k_ref, v_ref, g_ref, k_end_ref, v_end_ref, out_ref, up_ref, down_ref):
    extra = 4 * BLOCK // out_ref.shape[0]
    raw = jnp.concatenate([q_ref[...], k_ref[...], v_ref[...], g_ref[...]], axis=0)
    out_ref[:, :extra] = raw.reshape(out_ref.shape[0], extra, BLOCK)
    out_ref[:, extra:] = asked_ref[...]
    up_ref[0], up_ref[1] = k_end_ref[...], v_end_ref[...]
    down_ref[0], down_ref[1] = k_ref[...], v_ref[...]


def gather_kernel(wanted_ref, kv_ref, *refs):
    out_ref = refs[-1]

    def copy(d, _):
        for r in range(CAP):
            out_ref[d, r * BLOCK : (r + 1) * BLOCK] = kv_ref[wanted_ref[CAP * d + r]]
        for piece_ref in refs[:-1]:
            out_ref[d, CAP * BLOCK :] = piece_ref[...]
        return 0

    lax.fori_loop(0, out_ref.shape[0], copy, 0, unroll=2)


def query_pair(qg):
    low = low_lanes(qg.shape)
    return jnp.concatenate(
        [jnp.where(low, qg * SCALE, 0.0).astype(BF16), jnp.where(low, 0.0, qg).astype(BF16)], axis=0
    )


def main0_kernel(
    slot_ref, edge_ref, qg_ref, kv_ref, low_ref, high_ref, three_ref, raw_ref, stats_ref,
    od_ref, back_ref, acc_ref, side_ref, col_ref, pad_ref, ret_ref,
):
    attend(
        0, slot_ref, edge_ref, qg_ref, kv_ref, low_ref, high_ref, three_ref, raw_ref,
        od_ref, ret_ref, acc_ref, side_ref, col_ref, pad_ref,
    )

    def collect(d, _):
        for r in range(CAP):
            back_ref[d, r * BLOCK : (r + 1) * BLOCK] = ret_ref[CAP * d + r]
        back_ref[d, CAP * BLOCK :] = stats_ref[...]
        return 0

    lax.fori_loop(0, back_ref.shape[0], collect, 0)


def main1_kernel(
    slot_ref, edge_ref, qg_ref, kv_ref, low_ref, high_ref, three_ref, raw_ref, col0_ref,
    od_ref, back_ref, late_ref, acc_ref, side_ref, pad_ref, ret_ref, col_ref,
):
    shards, early = back_ref.shape[0], CAP * BLOCK - LATE
    half, extra = shards // 2, back_ref.shape[1] - early
    attend(
        1, slot_ref, edge_ref, qg_ref, kv_ref, low_ref, high_ref, three_ref, raw_ref,
        od_ref, ret_ref, acc_ref, side_ref, col_ref, pad_ref,
    )

    def collect(d, _):
        back_ref[d, :BLOCK] = ret_ref[CAP * d]
        back_ref[d, BLOCK : 2 * BLOCK] = ret_ref[CAP * d + 1]
        late_ref[d, :LATE] = ret_ref[CAP * d + 2]
        return 0

    lax.fori_loop(0, shards, collect, 0)
    parts = jnp.concatenate([col0_ref[...].astype(BF16), col_ref[...].astype(BF16)], axis=0)
    back_ref[:half, early:] = jnp.zeros((half, extra, BLOCK), BF16)
    back_ref[half:, early:] = parts.reshape(half, extra, BLOCK)
    late_ref[:, LATE:] = jnp.zeros((shards, extra, BLOCK), BF16)


def attend(
    head, slot_ref, edge_ref, qg_ref, kv_ref, low_ref, high_ref, far_ref, raw_ref,
    od_ref, ret_ref, acc_ref, side_ref, col_ref, pad_ref,
):
    blocks = qg_ref.shape[0]
    is_first, is_last = edge_ref[0], edge_ref[1]
    first = join(raw_ref[BLOCK : 2 * BLOCK], raw_ref[2 * BLOCK : 3 * BLOCK])[head]
    pad_ref[0] = join(low_ref[0], low_ref[1])[head]
    pad_ref[blocks + 1] = join(high_ref[0], high_ref[1])[head]
    pad_ref[1 : blocks + 1] = kv_ref[...]
    acc_ref[...] = jnp.zeros_like(acc_ref)
    ret_ref[...] = jnp.zeros_like(ret_ref)
    col_ref[...] = jnp.zeros_like(col_ref)

    def step(j, _):
        slot0, slot1 = slot_ref[2 * j], slot_ref[2 * j + 1]
        keep = 1.0 - ((j == 0) & (is_first == 1)).astype(F32)
        qg = qg_ref[j].astype(F32) * keep
        pair = query_pair(qg)
        window = pad_ref[pl.ds(j, 3)].reshape(3 * BLOCK, BLOCK)
        far0 = far_ref[slot0 // CAP, pl.ds(pl.multiple_of(slot0 % CAP * BLOCK, BLOCK), BLOCK)]
        far1 = far_ref[slot1 // CAP, pl.ds(pl.multiple_of(slot1 % CAP * BLOCK, BLOCK), BLOCK)]
        kv = jnp.concatenate([window, far0, far1, first], axis=0)
        both = dot(kv, pair, 1, 1)
        scores, gw = both[:, :BLOCK], both[:, BLOCK:]
        drop = (j == blocks - 1) & (is_last == 1)
        bias = jnp.where(drop, -jnp.inf, 0.0).astype(F32)
        scores = jnp.concatenate(
            [scores[: 2 * BLOCK], scores[2 * BLOCK : 3 * BLOCK] + bias, scores[3 * BLOCK :]], axis=0
        )
        peak = jnp.max(scores, axis=0, keepdims=True)
        expo = jnp.exp2((scores - peak) * LOG2E)
        weights = expo * (1.0 / jnp.sum(expo, axis=0, keepdims=True))
        wlow = weights.astype(BF16)
        kvt = kv.T
        out_t = dot(kvt, wlow, 1, 0)
        rounded = out_t.astype(BF16).astype(F32)
        row_dot = jnp.sum((rounded * qg.T)[HEAD_DIM:], axis=0, keepdims=True)
        ds = (weights * (gw - row_dot)).astype(BF16)
        dq_t = dot(kvt, ds, 1, 0)
        od_t = jnp.concatenate([dq_t[:HEAD_DIM] * SCALE, out_t[HEAD_DIM:]], axis=0)
        od_ref[j] = od_t.T.astype(BF16)
        terms = dot(jnp.concatenate([ds, wlow], axis=1), pair, 1, 0)
        acc_ref[pl.ds(j, 3)] += terms[: 3 * BLOCK].reshape(3, BLOCK, BLOCK)
        ret_ref[slot0] = terms[3 * BLOCK : 4 * BLOCK].astype(BF16)
        ret_ref[slot1] = terms[4 * BLOCK : 5 * BLOCK].astype(BF16)
        col_ref[...] += terms[5 * BLOCK :]
        return 0

    lax.fori_loop(0, blocks, step, 0)
    side_ref[0] = acc_ref[0].astype(BF16)
    side_ref[1] = acc_ref[blocks + 1].astype(BF16)


def raw_query(raw_ref):
    return join(raw_ref[:BLOCK], raw_ref[3 * BLOCK :])


def two_parts(x):
    high = x.astype(BF16)
    return high, (x - high.astype(F32)).astype(BF16)


def row_forward_kernel(raw_ref, kv0_ref, kv1_ref, stats_ref, peak_ref, out_ref, grad_ref, *, chunk):
    rows = []
    for h, kv_ref in enumerate((kv0_ref, kv1_ref)):
        qg = raw_query(raw_ref)[h].astype(F32)
        pair = query_pair(qg)

        def step(c, carry, kv_ref=kv_ref, pair=pair):
            peak, total, sums = carry
            kv = kv_ref[pl.ds(pl.multiple_of(c * chunk, chunk), chunk)]
            both = dot(kv, pair, 1, 1)
            scores = both[:, :BLOCK]
            new = jnp.maximum(peak, jnp.max(scores, axis=0, keepdims=True))
            shrink = jnp.exp2((peak - new) * LOG2E)
            expo = jnp.exp2((scores - new) * LOG2E)
            total = total * shrink + jnp.sum(expo, axis=0, keepdims=True)
            parts = [*two_parts(expo), *two_parts(expo * both[:, BLOCK:])]
            got = dot(kv.T, jnp.concatenate(parts, axis=1), 1, 0)
            got = [got[:, i * BLOCK : (i + 1) * BLOCK] for i in range(4)]
            sums = [sums[i] * shrink + got[2 * i] + got[2 * i + 1] for i in range(2)]
            return new, total, sums

        start = (
            jnp.full((1, BLOCK), -jnp.inf, F32),
            jnp.zeros((1, BLOCK), F32),
            [jnp.zeros((BLOCK, BLOCK), F32)] * 2,
        )
        peak, total, sums = lax.fori_loop(0, kv_ref.shape[0] // chunk, step, start)
        point = peak.astype(BF16)
        shift = jnp.exp2((peak - point.astype(F32)) * LOG2E)
        out_ref[h], grad_ref[h] = sums[0] * shift, sums[1] * shift
        row_dot = jnp.sum((sums[0] * shift * qg.T)[HEAD_DIM:], axis=0, keepdims=True)
        rows += [point, *two_parts(total * shift), *two_parts(row_dot)]
        peak_ref[h : h + 1] = point.astype(F32)
    rows = [r.astype(F32) for r in rows] + [jnp.zeros((6, BLOCK), F32)]
    stats_ref[...] = jnp.concatenate(rows, axis=0).astype(BF16)


def merged(all_ref, h):
    row = [all_ref[:, 5 * h + i].astype(F32) for i in range(5)]
    peak = jnp.max(row[0], axis=0, keepdims=True)
    grow = jnp.exp2((row[0] - peak) * LOG2E)
    scale = 1.0 / jnp.sum((row[1] + row[2]) * grow, axis=0, keepdims=True)
    return peak, scale, jnp.sum((row[3] + row[4]) * grow, axis=0, keepdims=True) * scale


def row_kernel(all_ref, peak_ref, out_ref, grad_ref, _, sent_ref):
    parts = []
    for h in range(2):
        peak, scale, row_dot = merged(all_ref, h)
        factor = jnp.exp2((peak_ref[h : h + 1] - peak) * LOG2E) * scale
        sums = out_ref[h] * factor
        dq = (grad_ref[h] * factor - sums * row_dot) * SCALE
        parts.append(jnp.concatenate([dq[:HEAD_DIM], sums[HEAD_DIM:]], axis=0).T.astype(BF16))
    sent_ref[...] = jnp.concatenate(parts, axis=0).reshape(sent_ref.shape)


def row_backward_kernel(raw_ref, kv0_ref, kv1_ref, all_ref, far0_ref, far1_ref, *, chunk):
    for h, (kv_ref, far_ref) in enumerate(((kv0_ref, far0_ref), (kv1_ref, far1_ref))):
        pair = query_pair(raw_query(raw_ref)[h].astype(F32))
        peak, scale, row_dot = merged(all_ref, h)

        def step(c, _, kv_ref=kv_ref, far_ref=far_ref, pair=pair, peak=peak, scale=scale, row_dot=row_dot):
            rows = pl.ds(pl.multiple_of(c * chunk, chunk), chunk)
            both = dot(kv_ref[rows], pair, 1, 1)
            weights = jnp.exp2((both[:, :BLOCK] - peak) * LOG2E) * scale
            ds = (weights * (both[:, BLOCK:] - row_dot)).astype(BF16)
            far_ref[rows] = dot(jnp.concatenate([ds, weights.astype(BF16)], axis=1), pair, 1, 0)
            return 0

        lax.fori_loop(0, kv_ref.shape[0] // chunk, step, 0)


def add_slots(tot_ref, wanted_ref, three_ref):
    def add(d, _):
        for r in range(CAP):
            tot_ref[wanted_ref[CAP * d + r]] += three_ref[d, r * BLOCK : (r + 1) * BLOCK].astype(F32)
        return 0

    lax.fori_loop(0, three_ref.shape[0], add, 0)


def own_rows(h, tot_ref, acc_ref, far_ref, left_ref, right_ref):
    blocks = tot_ref.shape[0]
    tot_ref[...] = acc_ref[1 : blocks + 1] + far_ref[...].reshape(tot_ref.shape)
    tot_ref[blocks - 1] += right_ref[h].astype(F32)
    tot_ref[0] += left_ref[h].astype(F32)


def total0_kernel(
    wanted_ref, acc_ref, far_ref, left_ref, right_ref, three_ref, out_ref, block_ref, tot_ref
):
    own_rows(0, tot_ref, acc_ref, far_ref, left_ref, right_ref)
    add_slots(tot_ref, wanted_ref, three_ref)
    block_ref[...] = tot_ref[0]
    out_ref[...] = tot_ref[...].astype(BF16)


def sum_kernel(parts_ref, _, out_ref):
    total = jnp.sum(parts_ref[...].astype(F32), axis=0, keepdims=True).astype(BF16)
    out_ref[...] = jnp.broadcast_to(total, out_ref.shape)


def total1_kernel(wanted_ref, acc_ref, far_ref, left_ref, right_ref, back_ref, tot_ref):
    own_rows(1, tot_ref, acc_ref, far_ref, left_ref, right_ref)

    def add(d, _):
        for r in range(CAP - 1):
            got = back_ref[d, r * BLOCK : (r + 1) * BLOCK]
            tot_ref[wanted_ref[CAP * d + r]] += got.astype(F32)
        return 0

    lax.fori_loop(0, back_ref.shape[0], add, 0)


def last_kernel(
    wanted_ref, edge_ref, part_ref, late_ref, head0_ref, block_ref, att_ref, dq_ref,
    dk_ref, dv_ref, att_out, dq_out, add_ref,
):
    step, count = pl.program_id(0), dk_ref.shape[0]

    @pl.when(step == 0)
    def _():
        add_ref[...] = jnp.zeros_like(add_ref)

        def add(d, _):
            add_ref[wanted_ref[CAP * d + CAP - 1]] += late_ref[d, :LATE].astype(F32)
            return 0

        lax.fori_loop(0, late_ref.shape[0], add, 0)
        is_first = edge_ref[0] == 1
        root = late_ref[:, LATE:].reshape(4 * BLOCK, BLOCK).astype(F32)
        root = [root[i * BLOCK : (i + 1) * BLOCK] for i in range(4)]
        add_ref[0] += root[3] * edge_ref[0].astype(F32)
        dk_ref[0], dv_ref[0] = join(
            block_ref[...] + root[2] * edge_ref[0].astype(F32), part_ref[0] + add_ref[0]
        )
        for new, old_ref, out_ref in zip(join(root[0], root[1]), (dq_ref, att_ref), (dq_out, att_out)):
            out_ref[...] = jnp.where(is_first, new.astype(F32), old_ref[...].astype(F32)).astype(BF16)

    for b in range(count):
        at = step * count + b

        @pl.when(at > 0)
        def _(b=b, at=at):
            dk_ref[b], dv_ref[b] = join(head0_ref[b], part_ref[b] + add_ref[at])


def unpack_kernel(od0_ref, od1_ref, att_ref, dq_ref):
    def write(b, _):
        dq_ref[b], att_ref[b] = join(od0_ref[b], od1_ref[b])
        return 0

    lax.fori_loop(0, od0_ref.shape[0], write, 0)


def in_hbm(x):
    return pltpu.with_memory_space_constraint(x, pltpu.HBM)


def call(kernel, outs, operands, smem=0, scratch=(), us=2, loose=(), free=False):
    return pl.pallas_call(
        kernel,
        out_shape=[jax.ShapeDtypeStruct(s, d) if free else pltpu.HBM(s, d) for s, d in outs],
        in_specs=[in_smem] * smem + [in_vmem] * (len(operands) - smem),
        out_specs=[in_vmem] * len(outs),
        scratch_shapes=[pltpu.VMEM(s, d) for s, d in scratch],
        compiler_params=params(),
        cost_estimate=pl.CostEstimate(flops=us * 10**9, transcendentals=0, bytes_accessed=10**6),
    )(*(x if i < smem or i in loose else in_hbm(x) for i, x in enumerate(operands)))


def exchange(blocks):
    return lax.all_to_all(blocks, "seq", split_axis=0, concat_axis=0, tiled=True)


def after(x, done):
    return lax.optimization_barrier((x, done))


def per_device(query, key, value, grad_out, random_blocks):
    shards, here = lax.axis_size("seq"), lax.axis_index("seq")
    rows = query.shape[0]
    blocks = rows // BLOCK
    slots = shards * CAP
    extra = 4 * BLOCK // shards
    tile = (BLOCK, BLOCK)
    grid = (blocks, *tile)
    forward = [(i, i + 1) for i in range(shards - 1)]
    backward = [(i + 1, i) for i in range(shards - 1)]

    named = random_blocks.reshape(-1)
    owners, inner = named // blocks, named % blocks
    places = jnp.arange(named.shape[0])
    same = (owners[:, None] == owners[None, :]) & (places[None, :] < places[:, None])
    slot_of = owners * CAP + jnp.sum(same.astype(jnp.int32), axis=1)
    asked = jnp.sum(
        jnp.where(slot_of[None, :] == jnp.arange(slots)[:, None], inner[None, :], 0), axis=1
    ).reshape(shards, 1, CAP)
    asked = jnp.pad(asked.astype(BF16), ((0, 0), (0, 15), (0, BLOCK - CAP)))
    top = pl.BlockSpec(tile, lambda i: (0, 0))
    end = pl.BlockSpec(tile, lambda i: (blocks - 1, 0))
    query, key, value, grad_out = (in_hbm(x) for x in (query, key, value, grad_out))
    message, up, down = pl.pallas_call(
        ask_kernel,
        grid=(1,),
        out_shape=[
            pltpu.HBM((shards, extra + 16, BLOCK), BF16),
            pltpu.HBM((2, *tile), BF16),
            pltpu.HBM((2, *tile), BF16),
        ],
        in_specs=[pl.BlockSpec(asked.shape, lambda i: (0, 0, 0)), top, top, top, top, end, end],
        out_specs=[
            pl.BlockSpec((shards, extra + 16, BLOCK), lambda i: (0, 0, 0)),
            pl.BlockSpec((2, *tile), lambda i: (0, 0, 0)),
            pl.BlockSpec((2, *tile), lambda i: (0, 0, 0)),
        ],
        compiler_params=params(),
    )(asked, query, key, value, grad_out, key, value)
    got = exchange(message)
    wanted = got[:, extra, :CAP].astype(jnp.int32).reshape(-1)
    edge = jnp.stack([here == 0, here == shards - 1]).astype(jnp.int32)

    chunk = 512
    part = pl.BlockSpec((chunk, BLOCK), lambda i: (i, 0))

    def pack(a, b):
        return pl.pallas_call(
            pack_kernel,
            grid=(rows // chunk,),
            out_shape=[pltpu.HBM((rows, BLOCK), BF16)] * 2,
            in_specs=[part] * 2,
            out_specs=[part] * 2,
            compiler_params=params(),
        )(a, b)

    kv0, kv1 = pack(key, value)
    steps = 4

    def gather(kv, *pieces):
        (sent,) = call(
            gather_kernel,
            [((shards, CAP * BLOCK + extra * len(pieces), BLOCK), BF16)],
            (wanted, kv.reshape(grid), *pieces),
            smem=1,
            loose=(2,),
        )
        return sent

    three0 = exchange(gather(kv0, got[0, :extra]))
    sent1 = gather(kv1)
    query, grad_out, up, down, sent1 = lax.optimization_barrier((query, grad_out, up, down, sent1))
    qg0, qg1 = pack(in_hbm(query), in_hbm(grad_out))
    low = lax.ppermute(up, "seq", forward)
    high = lax.ppermute(down, "seq", backward)
    sent1, three0, low, high = lax.optimization_barrier((sent1, three0, low, high))
    three1 = exchange(sent1)
    first = three0[:, CAP * BLOCK :].reshape(4 * BLOCK, BLOCK)
    stats, peak, sums, grads = call(
        functools.partial(row_forward_kernel, chunk=chunk),
        [((16, BLOCK), BF16), ((2, BLOCK), F32), ((2, *tile), F32), ((2, *tile), F32)],
        (first, kv0, kv1),
        us=14,
        loose=(0,),
    )
    padded = ((blocks + 2, *tile), BF16)
    returns = ((slots, *tile), BF16)
    od0, back0, acc0, side0, col0 = call(
        main0_kernel,
        [
            (grid, BF16),
            ((shards, CAP * BLOCK + extra, BLOCK), BF16),
            ((blocks + 2, *tile), F32),
            ((2, *tile), BF16),
            (tile, F32),
        ],
        (slot_of, edge, qg0.reshape(grid), kv0.reshape(grid), low, high, three0, first, stats),
        smem=2,
        loose=(4, 5, 6, 7, 8),
        scratch=[padded, returns],
        us=40,
    )
    back0, three1 = after(back0, three1)
    back0 = exchange(back0)
    early = CAP * BLOCK - LATE
    od1, back1, late1, acc1, side1 = call(
        main1_kernel,
        [
            (grid, BF16),
            ((shards, early + extra, BLOCK), BF16),
            ((shards, LATE + extra, BLOCK), BF16),
            ((blocks + 2, *tile), F32),
            ((2, *tile), BF16),
        ],
        (slot_of, edge, qg1.reshape(grid), kv1.reshape(grid), low, high, three1, first, col0),
        smem=2,
        loose=(4, 5, 6, 7),
        scratch=[padded, returns, (tile, F32)],
        us=40,
    )
    left = lax.ppermute(jnp.stack([side0[1], side1[1]]), "seq", forward)
    right = lax.ppermute(jnp.stack([side0[0], side1[0]]), "seq", backward)
    back1, back0, left, right = lax.optimization_barrier((back1, back0, left, right))
    full = lambda shape: pl.BlockSpec(shape, lambda i: (0,) * len(shape))
    behind = pl.BlockSpec((shards, extra, BLOCK), lambda i: (0, CAP * BLOCK // extra, 0))
    ours = pl.BlockSpec((shards // 2, extra, BLOCK), lambda i: (0, early // extra, 0))
    back1 = pl.pallas_call(
        row_kernel,
        grid=(1,),
        out_shape=pltpu.HBM(back1.shape, BF16),
        in_specs=[behind, full((2, BLOCK)), full((2, *tile)), full((2, *tile)), ours],
        out_specs=ours,
        input_output_aliases={4: 0},
        compiler_params=params(),
    )(back0, peak, sums, grads, in_hbm(back1))
    back1 = exchange(back1)
    far0, far1 = pl.pallas_call(
        functools.partial(row_backward_kernel, chunk=chunk),
        grid=(1,),
        out_shape=[pltpu.HBM((rows, BLOCK), F32)] * 2,
        in_specs=[full((4 * BLOCK, BLOCK)), full((rows, BLOCK)), full((rows, BLOCK)), behind],
        out_specs=[full((rows, BLOCK))] * 2,
        compiler_params=params(),
        cost_estimate=pl.CostEstimate(flops=8 * 10**9, transcendentals=0, bytes_accessed=10**6),
    )(first, in_hbm(kv0), in_hbm(kv1), back0)
    attended, grad_query = call(unpack_kernel, [(grid, BF16)] * 2, (od0, od1), us=4)
    whole = [(grid, F32)]
    head0, block0 = call(
        total0_kernel,
        [(grid, BF16), (tile, F32)],
        (wanted, acc0, far0, left, right, back0),
        smem=1,
        scratch=whole,
        us=6,
        loose=(3, 4, 5),
    )
    back1, far1, head0, block0 = lax.optimization_barrier((back1, far1, head0, block0))
    pieces = pl.BlockSpec((shards, extra, BLOCK), lambda i: (0, early // extra, 0))
    tail = pl.BlockSpec((shards, extra, BLOCK), lambda i: (0, LATE // extra, 0))
    late1 = pl.pallas_call(
        sum_kernel,
        grid=(1,),
        out_shape=pltpu.HBM(late1.shape, BF16),
        in_specs=[pieces, pl.BlockSpec((shards, extra, BLOCK), lambda i: (0, LATE // extra, 0))],
        out_specs=tail,
        input_output_aliases={1: 0},
        compiler_params=params(),
    )(back1, in_hbm(late1))
    late1 = exchange(late1)
    (part1,) = call(
        total1_kernel,
        whole,
        (wanted, acc1, far1, left, right, back1),
        smem=1,
        us=4,
        loose=(3, 4, 5),
    )
    out_block = pl.BlockSpec((blocks // steps, *tile), lambda i: (i, 0, 0))
    attended, grad_query = (in_hbm(x.reshape(rows, BLOCK)) for x in (attended, grad_query))
    grad_key, grad_value, attended, grad_query = pl.pallas_call(
        last_kernel,
        grid=(steps,),
        out_shape=[pltpu.HBM(grid, BF16)] * 2 + [pltpu.HBM((rows, BLOCK), BF16)] * 2,
        in_specs=[in_smem, in_smem, out_block, full(late1.shape), out_block, full(tile), top, top],
        out_specs=[out_block, out_block, top, top],
        input_output_aliases={6: 2, 7: 3},
        scratch_shapes=[pltpu.VMEM(grid, F32)],
        compiler_params=params(),
        cost_estimate=pl.CostEstimate(flops=4 * 10**9, transcendentals=0, bytes_accessed=10**6),
    )(wanted, edge, in_hbm(part1), late1, in_hbm(head0), in_hbm(block0), attended, grad_query)
    return attended, grad_query, grad_key.reshape(rows, BLOCK), grad_value.reshape(rows, BLOCK)


def solution(mesh):
    split = P("seq", "head")
    return jax.shard_map(
        per_device,
        mesh=mesh,
        in_specs=(split, split, split, split, P("seq", None)),
        out_specs=(split, split, split, split),
        check_vma=False,
    )
```

```python
import functools
import math

import jax
import jax.numpy as jnp
from jax import lax
from jax.experimental import pallas as pl
from jax.experimental.pallas import tpu as pltpu
from jax.sharding import PartitionSpec as P

HEAD_DIM = 64
BLOCK = 128
CAP = 3
LOG2E = math.log2(math.e)
SCALE = HEAD_DIM**-0.5
F32 = jnp.float32
BF16 = jnp.bfloat16
VMEM_LIMIT = 28 * 1024 * 1024

in_vmem = pl.BlockSpec(memory_space=pltpu.VMEM)
in_smem = pl.BlockSpec(memory_space=pltpu.SMEM)


def params():
    return pltpu.CompilerParams(vmem_limit_bytes=VMEM_LIMIT)


def dot(a, b, a_dim, b_dim):
    return lax.dot_general(a, b, (((a_dim,), (b_dim,)), ((), ())), preferred_element_type=F32)


def low_lanes(shape):
    return lax.broadcasted_iota(jnp.int32, shape, len(shape) - 1) < HEAD_DIM


def join(a, b):
    a, b = a.astype(F32), b.astype(F32)
    low = low_lanes(a.shape)
    axis = a.ndim - 1
    first = jnp.where(low, a, pltpu.roll(b, HEAD_DIM, axis))
    second = jnp.where(low, pltpu.roll(a, HEAD_DIM, axis), b)
    return first.astype(BF16), second.astype(BF16)


def pack_kernel(a_ref, b_ref, head0_ref, head1_ref):
    head0_ref[...], head1_ref[...] = join(a_ref[...], b_ref[...])


def ask_kernel(asked_ref, q_ref, k_ref, v_ref, g_ref, k_end_ref, v_end_ref, out_ref, up_ref, down_ref):
    extra = 4 * BLOCK // out_ref.shape[0]
    raw = jnp.concatenate([q_ref[...], k_ref[...], v_ref[...], g_ref[...]], axis=0)
    out_ref[:, :extra] = raw.reshape(out_ref.shape[0], extra, BLOCK)
    out_ref[:, extra:] = asked_ref[...]
    up_ref[0], up_ref[1] = k_end_ref[...], v_end_ref[...]
    down_ref[0], down_ref[1] = k_ref[...], v_ref[...]


def gather0_kernel(wanted_ref, kv_ref, piece_ref, out_ref):
    count = out_ref.shape[0]
    start = pl.program_id(0) * count
    for d in range(count):
        out_ref[d, :BLOCK] = kv_ref[wanted_ref[CAP * (start + d)]]
        out_ref[d, BLOCK:] = piece_ref[...]


def gather0_rest_kernel(wanted_ref, kv_ref, out_ref):
    def copy(d, _):
        out_ref[d, :BLOCK] = kv_ref[wanted_ref[CAP * d + 1]]
        out_ref[d, BLOCK:] = kv_ref[wanted_ref[CAP * d + 2]]
        return 0

    lax.fori_loop(0, out_ref.shape[0], copy, 0, unroll=2)


def gather1_kernel(wanted_ref, kv_ref, piece_ref, out_ref):
    def copy(d, _):
        for r in range(CAP):
            out_ref[d, r * BLOCK : (r + 1) * BLOCK] = kv_ref[wanted_ref[CAP * d + r]]
        out_ref[d, CAP * BLOCK :] = piece_ref[...]
        return 0

    lax.fori_loop(0, out_ref.shape[0], copy, 0, unroll=2)


def query_pair(qg):
    low = low_lanes(qg.shape)
    return jnp.concatenate(
        [jnp.where(low, qg * SCALE, 0.0).astype(BF16), jnp.where(low, 0.0, qg).astype(BF16)], axis=0
    )


def main0_kernel(
    slot_ref, edge_ref, qg_ref, kv_ref, low_ref, high_ref, one_ref, two_ref, raw_ref,
    od_ref, back_ref, acc_ref, side_ref, col_ref, pad_ref, far_ref, ret_ref,
):
    shards = one_ref.shape[0]
    far_ref[:, :BLOCK] = one_ref[:, :BLOCK]
    far_ref[:, BLOCK:] = two_ref[...]
    attend(
        0, slot_ref, edge_ref, qg_ref, kv_ref, low_ref, high_ref, far_ref, raw_ref,
        od_ref, ret_ref, acc_ref, side_ref, col_ref, pad_ref,
    )

    def collect(d, _):
        for r in range(CAP):
            back_ref[d, r * BLOCK : (r + 1) * BLOCK] = ret_ref[CAP * d + r]
        return 0

    lax.fori_loop(0, shards, collect, 0)


def main1_kernel(
    slot_ref, edge_ref, qg_ref, kv_ref, low_ref, high_ref, three_ref, raw_ref, row_ref, col0_ref,
    od_ref, two_ref, one_ref, acc_ref, side_ref, pad_ref, ret_ref, col_ref,
):
    shards, extra = one_ref.shape[0], one_ref.shape[1] - BLOCK

    attend(
        1, slot_ref, edge_ref, qg_ref, kv_ref, low_ref, high_ref, three_ref, raw_ref,
        od_ref, ret_ref, acc_ref, side_ref, col_ref, pad_ref,
    )

    def collect(d, _):
        two_ref[d, :BLOCK] = ret_ref[CAP * d]
        two_ref[d, BLOCK : 2 * BLOCK] = ret_ref[CAP * d + 1]
        one_ref[d, :BLOCK] = ret_ref[CAP * d + 2]
        return 0

    lax.fori_loop(0, shards, collect, 0)
    parts = [row_ref[0], row_ref[1], col0_ref[...], col_ref[...]]
    parts = jnp.concatenate([x.astype(BF16) for x in parts], axis=0)
    two_ref[:, 2 * BLOCK :] = parts.reshape(shards, extra, BLOCK)
    one_ref[:, BLOCK:] = jnp.zeros((shards, extra, BLOCK), BF16)


def attend(
    head, slot_ref, edge_ref, qg_ref, kv_ref, low_ref, high_ref, far_ref, raw_ref,
    od_ref, ret_ref, acc_ref, side_ref, col_ref, pad_ref,
):
    blocks = qg_ref.shape[0]
    is_first, is_last = edge_ref[0], edge_ref[1]
    first = join(raw_ref[BLOCK : 2 * BLOCK], raw_ref[2 * BLOCK : 3 * BLOCK])[head]
    pad_ref[0] = join(low_ref[0], low_ref[1])[head]
    pad_ref[blocks + 1] = join(high_ref[0], high_ref[1])[head]
    pad_ref[1 : blocks + 1] = kv_ref[...]
    acc_ref[...] = jnp.zeros_like(acc_ref)
    ret_ref[...] = jnp.zeros_like(ret_ref)
    col_ref[...] = jnp.zeros_like(col_ref)

    def step(j, _):
        slot0, slot1 = slot_ref[2 * j], slot_ref[2 * j + 1]
        keep = 1.0 - ((j == 0) & (is_first == 1)).astype(F32)
        qg = qg_ref[j].astype(F32) * keep
        pair = query_pair(qg)
        window = pad_ref[pl.ds(j, 3)].reshape(3 * BLOCK, BLOCK)
        far0 = far_ref[slot0 // CAP, pl.ds(pl.multiple_of(slot0 % CAP * BLOCK, BLOCK), BLOCK)]
        far1 = far_ref[slot1 // CAP, pl.ds(pl.multiple_of(slot1 % CAP * BLOCK, BLOCK), BLOCK)]
        kv = jnp.concatenate([window, far0, far1, first], axis=0)
        both = dot(kv, pair, 1, 1)
        scores, gw = both[:, :BLOCK], both[:, BLOCK:]
        drop = (j == blocks - 1) & (is_last == 1)
        bias = jnp.where(drop, -jnp.inf, 0.0).astype(F32)
        scores = jnp.concatenate(
            [scores[: 2 * BLOCK], scores[2 * BLOCK : 3 * BLOCK] + bias, scores[3 * BLOCK :]], axis=0
        )
        peak = jnp.max(scores, axis=0, keepdims=True)
        expo = jnp.exp2((scores - peak) * LOG2E)
        weights = expo * (1.0 / jnp.sum(expo, axis=0, keepdims=True))
        wlow = weights.astype(BF16)
        kvt = kv.T
        out_t = dot(kvt, wlow, 1, 0)
        rounded = out_t.astype(BF16).astype(F32)
        row_dot = jnp.sum((rounded * qg.T)[HEAD_DIM:], axis=0, keepdims=True)
        ds = (weights * (gw - row_dot)).astype(BF16)
        dq_t = dot(kvt, ds, 1, 0)
        od_t = jnp.concatenate([dq_t[:HEAD_DIM] * SCALE, out_t[HEAD_DIM:]], axis=0)
        od_ref[j] = od_t.T.astype(BF16)
        terms = dot(jnp.concatenate([ds, wlow], axis=1), pair, 1, 0)
        acc_ref[pl.ds(j, 3)] += terms[: 3 * BLOCK].reshape(3, BLOCK, BLOCK)
        ret_ref[slot0] = terms[3 * BLOCK : 4 * BLOCK].astype(BF16)
        ret_ref[slot1] = terms[4 * BLOCK : 5 * BLOCK].astype(BF16)
        col_ref[...] += terms[5 * BLOCK :]
        return 0

    lax.fori_loop(0, blocks, step, 0)
    side_ref[0] = acc_ref[0].astype(BF16)
    side_ref[1] = acc_ref[blocks + 1].astype(BF16)


def raw_query(raw_ref):
    return join(raw_ref[:BLOCK], raw_ref[3 * BLOCK :])


def two_parts(x):
    high = x.astype(BF16)
    return high, (x - high.astype(F32)).astype(BF16)


def row_forward_kernel(raw_ref, kv0_ref, kv1_ref, stats_ref, peak_ref, out_ref, *, chunk):
    rows = []
    for h, kv_ref in enumerate((kv0_ref, kv1_ref)):
        qg = raw_query(raw_ref)[h].astype(F32)
        query = query_pair(qg)[:BLOCK]

        def step(c, carry, kv_ref=kv_ref, query=query):
            peak, total, out = carry
            kv = kv_ref[pl.ds(pl.multiple_of(c * chunk, chunk), chunk)]
            scores = dot(kv, query, 1, 1)
            new = jnp.maximum(peak, jnp.max(scores, axis=0, keepdims=True))
            shrink = jnp.exp2((peak - new) * LOG2E)
            expo = jnp.exp2((scores - new) * LOG2E)
            total = total * shrink + jnp.sum(expo, axis=0, keepdims=True)
            out = out * shrink + dot(kv, expo.astype(BF16), 0, 0)
            return new, total, out

        start = (
            jnp.full((1, BLOCK), -jnp.inf, F32),
            jnp.zeros((1, BLOCK), F32),
            jnp.zeros((BLOCK, BLOCK), F32),
        )
        peak, total, out = lax.fori_loop(0, kv_ref.shape[0] // chunk, step, start)
        point = peak.astype(BF16)
        shift = jnp.exp2((peak - point.astype(F32)) * LOG2E)
        out = out * shift
        row_dot = jnp.sum((out * qg.T)[HEAD_DIM:], axis=0, keepdims=True)
        rows += [point, *two_parts(total * shift), *two_parts(row_dot)]
        peak_ref[h : h + 1] = point.astype(F32)
        out_ref[h] = out
    rows = [r.astype(F32) for r in rows] + [jnp.zeros((6, BLOCK), F32)]
    stats_ref[...] = jnp.concatenate(rows, axis=0).astype(BF16)


def row_backward_kernel(
    raw_ref, kv0_ref, kv1_ref, all_ref, peak_ref, out_ref, far0_ref, far1_ref, row_ref, *, chunk
):
    stats = all_ref[...].astype(F32)
    for h, (kv_ref, far_ref) in enumerate(((kv0_ref, far0_ref), (kv1_ref, far1_ref))):
        qg = raw_query(raw_ref)[h].astype(F32)
        pair = query_pair(qg)
        row = [stats[:, 5 * h + i] for i in range(5)]
        peak = jnp.max(row[0], axis=0, keepdims=True)
        grow = jnp.exp2((row[0] - peak) * LOG2E)
        scale = 1.0 / jnp.sum((row[1] + row[2]) * grow, axis=0, keepdims=True)
        row_dot = jnp.sum((row[3] + row[4]) * grow, axis=0, keepdims=True) * scale

        def step(c, dq_t, kv_ref=kv_ref, far_ref=far_ref, pair=pair, peak=peak, scale=scale, row_dot=row_dot):
            rows = pl.ds(pl.multiple_of(c * chunk, chunk), chunk)
            kv = kv_ref[rows]
            both = dot(kv, pair, 1, 1)
            weights = jnp.exp2((both[:, :BLOCK] - peak) * LOG2E) * scale
            ds = (weights * (both[:, BLOCK:] - row_dot)).astype(BF16)
            far_ref[rows] = dot(jnp.concatenate([ds, weights.astype(BF16)], axis=1), pair, 1, 0)
            return dq_t + dot(kv, ds, 0, 0)

        dq_t = lax.fori_loop(0, kv_ref.shape[0] // chunk, step, jnp.zeros((BLOCK, BLOCK), F32))
        out_t = out_ref[h] * (jnp.exp2((peak_ref[h : h + 1] - peak) * LOG2E) * scale)
        row_ref[h] = jnp.concatenate([dq_t[:HEAD_DIM] * SCALE, out_t[HEAD_DIM:]], axis=0).T


def add_slots(tot_ref, wanted_ref, back_ref, ranks):
    def add(d, _):
        for at, r in enumerate(ranks):
            tot_ref[wanted_ref[CAP * d + r]] += back_ref[d, at * BLOCK : (at + 1) * BLOCK].astype(F32)
        return 0

    lax.fori_loop(0, back_ref.shape[0], add, 0)


def own_rows(h, tot_ref, acc_ref, far_ref, left_ref, right_ref):
    blocks = tot_ref.shape[0]
    tot_ref[...] = acc_ref[1 : blocks + 1] + far_ref[...].reshape(tot_ref.shape)
    tot_ref[blocks - 1] += right_ref[h].astype(F32)
    tot_ref[0] += left_ref[h].astype(F32)


def total0_kernel(
    wanted_ref, acc_ref, far_ref, left_ref, right_ref, three_ref, out_ref, block_ref, tot_ref
):
    own_rows(0, tot_ref, acc_ref, far_ref, left_ref, right_ref)
    add_slots(tot_ref, wanted_ref, three_ref, range(CAP))
    block_ref[...] = tot_ref[0]
    out_ref[...] = tot_ref[...].astype(BF16)


def total1_kernel(wanted_ref, acc_ref, far_ref, left_ref, right_ref, two_ref, tot_ref):
    own_rows(1, tot_ref, acc_ref, far_ref, left_ref, right_ref)
    add_slots(tot_ref, wanted_ref, two_ref, range(2))


def last_kernel(
    wanted_ref, edge_ref, part_ref, late_ref, head0_ref, block_ref, att_ref, dq_ref,
    dk_ref, dv_ref, att_out, dq_out, add_ref,
):
    step, count = pl.program_id(0), dk_ref.shape[0]

    @pl.when(step == 0)
    def _():
        add_ref[...] = jnp.zeros_like(add_ref)

        def add(d, _):
            add_ref[wanted_ref[CAP * d + CAP - 1]] += late_ref[d, :BLOCK].astype(F32)
            return 0

        lax.fori_loop(0, late_ref.shape[0], add, 0)
        is_first = edge_ref[0] == 1
        root = late_ref[:, BLOCK:].reshape(4 * BLOCK, BLOCK).astype(F32)
        root = [root[i * BLOCK : (i + 1) * BLOCK] for i in range(4)]
        add_ref[0] += root[3] * edge_ref[0].astype(F32)
        dk_ref[0], dv_ref[0] = join(
            block_ref[...] + root[2] * edge_ref[0].astype(F32), part_ref[0] + add_ref[0]
        )
        for new, old_ref, out_ref in zip(join(root[0], root[1]), (dq_ref, att_ref), (dq_out, att_out)):
            out_ref[...] = jnp.where(is_first, new.astype(F32), old_ref[...].astype(F32)).astype(BF16)

    for b in range(count):
        at = step * count + b

        @pl.when(at > 0)
        def _(b=b, at=at):
            dk_ref[b], dv_ref[b] = join(head0_ref[b], part_ref[b] + add_ref[at])


def unpack_kernel(od0_ref, od1_ref, att_ref, dq_ref):
    def write(b, _):
        dq_ref[b], att_ref[b] = join(od0_ref[b], od1_ref[b])
        return 0

    lax.fori_loop(0, od0_ref.shape[0], write, 0)


def in_hbm(x):
    return pltpu.with_memory_space_constraint(x, pltpu.HBM)


def call(kernel, outs, operands, smem=0, scratch=(), us=2, loose=()):
    return pl.pallas_call(
        kernel,
        out_shape=[pltpu.HBM(s, d) for s, d in outs],
        in_specs=[in_smem] * smem + [in_vmem] * (len(operands) - smem),
        out_specs=[in_vmem] * len(outs),
        scratch_shapes=[pltpu.VMEM(s, d) for s, d in scratch],
        compiler_params=params(),
        cost_estimate=pl.CostEstimate(flops=us * 10**9, transcendentals=0, bytes_accessed=10**6),
    )(*(x if i < smem or i in loose else in_hbm(x) for i, x in enumerate(operands)))


def exchange(blocks):
    return lax.all_to_all(blocks, "seq", split_axis=0, concat_axis=0, tiled=True)


def after(x, done):
    return lax.optimization_barrier((x, done))


def per_device(query, key, value, grad_out, random_blocks):
    shards, here = lax.axis_size("seq"), lax.axis_index("seq")
    rows = query.shape[0]
    blocks = rows // BLOCK
    slots = shards * CAP
    extra = 4 * BLOCK // shards
    tile = (BLOCK, BLOCK)
    grid = (blocks, *tile)
    forward = [(i, i + 1) for i in range(shards - 1)]
    backward = [(i + 1, i) for i in range(shards - 1)]

    named = random_blocks.reshape(-1)
    owners, inner = named // blocks, named % blocks
    places = jnp.arange(named.shape[0])
    same = (owners[:, None] == owners[None, :]) & (places[None, :] < places[:, None])
    slot_of = owners * CAP + jnp.sum(same.astype(jnp.int32), axis=1)
    asked = jnp.sum(
        jnp.where(slot_of[None, :] == jnp.arange(slots)[:, None], inner[None, :], 0), axis=1
    ).reshape(shards, 1, CAP)
    asked = jnp.pad(asked.astype(BF16), ((0, 0), (0, 15), (0, BLOCK - CAP)))
    top = pl.BlockSpec(tile, lambda i: (0, 0))
    end = pl.BlockSpec(tile, lambda i: (blocks - 1, 0))
    query, key, value, grad_out = (in_hbm(x) for x in (query, key, value, grad_out))
    message, up, down = pl.pallas_call(
        ask_kernel,
        grid=(1,),
        out_shape=[
            pltpu.HBM((shards, extra + 16, BLOCK), BF16),
            pltpu.HBM((2, *tile), BF16),
            pltpu.HBM((2, *tile), BF16),
        ],
        in_specs=[pl.BlockSpec(asked.shape, lambda i: (0, 0, 0)), top, top, top, top, end, end],
        out_specs=[
            pl.BlockSpec((shards, extra + 16, BLOCK), lambda i: (0, 0, 0)),
            pl.BlockSpec((2, *tile), lambda i: (0, 0, 0)),
            pl.BlockSpec((2, *tile), lambda i: (0, 0, 0)),
        ],
        compiler_params=params(),
    )(asked, query, key, value, grad_out, key, value)
    got = exchange(message)
    wanted = got[:, extra, :CAP].astype(jnp.int32).reshape(-1)
    edge = jnp.stack([here == 0, here == shards - 1]).astype(jnp.int32)

    chunk = 512
    part = pl.BlockSpec((chunk, BLOCK), lambda i: (i, 0))

    def pack(a, b):
        return pl.pallas_call(
            pack_kernel,
            grid=(rows // chunk,),
            out_shape=[pltpu.HBM((rows, BLOCK), BF16)] * 2,
            in_specs=[part] * 2,
            out_specs=[part] * 2,
            compiler_params=params(),
        )(a, b)

    kv0, kv1 = pack(key, value)
    steps = 4
    one0 = pl.pallas_call(
        gather0_kernel,
        grid=(steps,),
        out_shape=pltpu.HBM((shards, BLOCK + extra, BLOCK), BF16),
        in_specs=[
            in_smem,
            pl.BlockSpec(grid, lambda i: (0, 0, 0)),
            pl.BlockSpec((extra, BLOCK), lambda i: (0, 0)),
        ],
        out_specs=pl.BlockSpec((shards // steps, BLOCK + extra, BLOCK), lambda i: (i, 0, 0)),
        compiler_params=params(),
    )(wanted, in_hbm(kv0.reshape(grid)), got[0, :extra])
    (two0,) = call(
        gather0_rest_kernel,
        [((shards, 2 * BLOCK, BLOCK), BF16)],
        (wanted, kv0.reshape(grid)),
        smem=1,
    )
    one0 = exchange(one0)
    query, grad_out, up, down, two0 = lax.optimization_barrier((query, grad_out, up, down, two0))
    qg0, qg1 = pack(in_hbm(query), in_hbm(grad_out))
    low = lax.ppermute(up, "seq", forward)
    high = lax.ppermute(down, "seq", backward)
    two0, one0, low, high = lax.optimization_barrier((two0, one0, low, high))
    two0 = exchange(two0)
    first = one0[:, BLOCK:].reshape(4 * BLOCK, BLOCK)
    stats, peak, partial = call(
        functools.partial(row_forward_kernel, chunk=chunk),
        [((16, BLOCK), BF16), ((2, BLOCK), F32), ((2, *tile), F32)],
        (first, kv0, kv1),
        us=8,
        loose=(0,),
    )
    (three1,) = call(
        gather1_kernel,
        [((shards, CAP * BLOCK + extra, BLOCK), BF16)],
        (wanted, kv1.reshape(grid), stats),
        smem=1,
        loose=(2,),
    )
    three1, two0 = after(three1, two0)
    three1 = exchange(three1)
    padded = ((blocks + 2, *tile), BF16)
    returns = ((slots, *tile), BF16)
    od0, back0, acc0, side0, col0 = call(
        main0_kernel,
        [
            (grid, BF16),
            ((shards, CAP * BLOCK, BLOCK), BF16),
            ((blocks + 2, *tile), F32),
            ((2, *tile), BF16),
            (tile, F32),
        ],
        (slot_of, edge, qg0.reshape(grid), kv0.reshape(grid), low, high, one0, two0, first),
        smem=2,
        loose=(4, 5, 6, 7, 8),
        scratch=[padded, ((shards, CAP * BLOCK, BLOCK), BF16), returns],
        us=38,
    )
    back0, three1 = after(back0, three1)
    back0 = exchange(back0)
    far0, far1, row_od = call(
        functools.partial(row_backward_kernel, chunk=chunk),
        [((rows, BLOCK), F32)] * 2 + [((2, *tile), F32)],
        (first, kv0, kv1, three1[:, CAP * BLOCK :], peak, partial),
        us=8,
        loose=(0, 3),
    )
    od1, two1, one1, acc1, side1 = call(
        main1_kernel,
        [
            (grid, BF16),
            ((shards, 2 * BLOCK + extra, BLOCK), BF16),
            ((shards, BLOCK + extra, BLOCK), BF16),
            ((blocks + 2, *tile), F32),
            ((2, *tile), BF16),
        ],
        (
            slot_of, edge, qg1.reshape(grid), kv1.reshape(grid), low, high, three1, first,
            row_od, col0,
        ),
        smem=2,
        loose=(4, 5, 6, 7),
        scratch=[padded, returns, (tile, F32)],
        us=38,
    )
    left = lax.ppermute(jnp.stack([side0[1], side1[1]]), "seq", forward)
    right = lax.ppermute(jnp.stack([side0[0], side1[0]]), "seq", backward)
    two1, back0, left, right = lax.optimization_barrier((two1, back0, left, right))
    two1 = exchange(two1)
    total = jnp.sum(two1[:, 2 * BLOCK :].astype(F32), axis=0).astype(BF16)
    one1 = one1.at[:, BLOCK:].set(jnp.broadcast_to(total, (shards, extra, BLOCK)))
    one1 = exchange(one1)
    attended, grad_query = call(unpack_kernel, [(grid, BF16)] * 2, (od0, od1), us=4)
    whole = [(grid, F32)]
    head0, block0 = call(
        total0_kernel,
        [(grid, BF16), (tile, F32)],
        (wanted, acc0, far0, left, right, back0),
        smem=1,
        scratch=whole,
        us=6,
        loose=(3, 4, 5),
    )
    (part1,) = call(
        total1_kernel,
        whole,
        (wanted, acc1, far1, left, right, two1),
        smem=1,
        us=4,
        loose=(3, 4, 5),
    )
    full = lambda shape: pl.BlockSpec(shape, lambda i: (0,) * len(shape))
    out_block = pl.BlockSpec((blocks // steps, *tile), lambda i: (i, 0, 0))
    attended, grad_query = (in_hbm(x.reshape(rows, BLOCK)) for x in (attended, grad_query))
    grad_key, grad_value, attended, grad_query = pl.pallas_call(
        last_kernel,
        grid=(steps,),
        out_shape=[pltpu.HBM(grid, BF16)] * 2 + [pltpu.HBM((rows, BLOCK), BF16)] * 2,
        in_specs=[in_smem, in_smem, out_block, full(one1.shape), out_block, full(tile), top, top],
        out_specs=[out_block, out_block, top, top],
        input_output_aliases={6: 2, 7: 3},
        scratch_shapes=[pltpu.VMEM(grid, F32)],
        compiler_params=params(),
        cost_estimate=pl.CostEstimate(flops=4 * 10**9, transcendentals=0, bytes_accessed=10**6),
    )(wanted, edge, in_hbm(part1), one1, in_hbm(head0), in_hbm(block0), attended, grad_query)
    return attended, grad_query, grad_key.reshape(rows, BLOCK), grad_value.reshape(rows, BLOCK)


def solution(mesh):
    split = P("seq", "head")
    return jax.shard_map(
        per_device,
        mesh=mesh,
        in_specs=(split, split, split, split, P("seq", None)),
        out_specs=(split, split, split, split),
        check_vma=False,
    )
```

```python
import functools
import math

import jax
import jax.numpy as jnp
from jax import lax
from jax.experimental import pallas as pl
from jax.experimental.pallas import tpu as pltpu
from jax.sharding import PartitionSpec as P

HEAD_DIM = 64
BLOCK = 128
CAP = 3
LOG2E = math.log2(math.e)
SCALE = HEAD_DIM**-0.5
F32 = jnp.float32
BF16 = jnp.bfloat16
VMEM_LIMIT = 28 * 1024 * 1024

in_vmem = pl.BlockSpec(memory_space=pltpu.VMEM)
in_smem = pl.BlockSpec(memory_space=pltpu.SMEM)


def params():
    return pltpu.CompilerParams(vmem_limit_bytes=VMEM_LIMIT)


def dot(a, b, a_dim, b_dim):
    return lax.dot_general(a, b, (((a_dim,), (b_dim,)), ((), ())), preferred_element_type=F32)


def low_lanes(shape):
    return lax.broadcasted_iota(jnp.int32, shape, len(shape) - 1) < HEAD_DIM


def join(a, b):
    a, b = a.astype(F32), b.astype(F32)
    low = low_lanes(a.shape)
    axis = a.ndim - 1
    first = jnp.where(low, a, pltpu.roll(b, HEAD_DIM, axis))
    second = jnp.where(low, pltpu.roll(a, HEAD_DIM, axis), b)
    return first.astype(BF16), second.astype(BF16)


def pack_kernel(a_ref, b_ref, head0_ref, head1_ref):
    head0_ref[...], head1_ref[...] = join(a_ref[...], b_ref[...])


def ask_kernel(asked_ref, q_ref, k_ref, v_ref, g_ref, k_end_ref, v_end_ref, out_ref, up_ref, down_ref):
    extra = 4 * BLOCK // out_ref.shape[0]
    raw = jnp.concatenate([q_ref[...], k_ref[...], v_ref[...], g_ref[...]], axis=0)
    out_ref[:, :extra] = raw.reshape(out_ref.shape[0], extra, BLOCK)
    out_ref[:, extra:] = asked_ref[...]
    up_ref[0], up_ref[1] = k_end_ref[...], v_end_ref[...]
    down_ref[0], down_ref[1] = k_ref[...], v_ref[...]


def gather0_kernel(wanted_ref, kv_ref, piece_ref, out_ref):
    def copy(d, _):
        out_ref[d, :BLOCK] = kv_ref[wanted_ref[CAP * d]]
        out_ref[d, BLOCK:] = piece_ref[...]
        return 0

    lax.fori_loop(0, out_ref.shape[0], copy, 0, unroll=4)


def gather0_rest_kernel(wanted_ref, kv_ref, out_ref):
    def copy(d, _):
        out_ref[d, :BLOCK] = kv_ref[wanted_ref[CAP * d + 1]]
        out_ref[d, BLOCK:] = kv_ref[wanted_ref[CAP * d + 2]]
        return 0

    lax.fori_loop(0, out_ref.shape[0], copy, 0, unroll=2)


def gather1_kernel(wanted_ref, kv_ref, piece_ref, out_ref):
    def copy(d, _):
        for r in range(CAP):
            out_ref[d, r * BLOCK : (r + 1) * BLOCK] = kv_ref[wanted_ref[CAP * d + r]]
        out_ref[d, CAP * BLOCK :] = piece_ref[...]
        return 0

    lax.fori_loop(0, out_ref.shape[0], copy, 0, unroll=2)


def query_pair(qg):
    low = low_lanes(qg.shape)
    return jnp.concatenate(
        [jnp.where(low, qg * SCALE, 0.0).astype(BF16), jnp.where(low, 0.0, qg).astype(BF16)], axis=0
    )


def main0_kernel(
    slot_ref, edge_ref, qg_ref, kv_ref, low_ref, high_ref, one_ref, two_ref, raw_ref,
    od_ref, back_ref, acc_ref, side_ref, col_ref, pad_ref, far_ref, ret_ref,
):
    shards = one_ref.shape[0]
    far_ref[:, :BLOCK] = one_ref[:, :BLOCK]
    far_ref[:, BLOCK:] = two_ref[...]
    attend(
        0, slot_ref, edge_ref, qg_ref, kv_ref, low_ref, high_ref, far_ref, raw_ref,
        od_ref, ret_ref, acc_ref, side_ref, col_ref, pad_ref,
    )

    def collect(d, _):
        for r in range(CAP):
            back_ref[d, r * BLOCK : (r + 1) * BLOCK] = ret_ref[CAP * d + r]
        return 0

    lax.fori_loop(0, shards, collect, 0)


def main1_kernel(
    slot_ref, edge_ref, qg_ref, kv_ref, low_ref, high_ref, three_ref, raw_ref, row_ref, col0_ref,
    od_ref, two_ref, one_ref, acc_ref, side_ref, pad_ref, ret_ref, col_ref,
):
    shards, extra = one_ref.shape[0], one_ref.shape[1] - BLOCK

    attend(
        1, slot_ref, edge_ref, qg_ref, kv_ref, low_ref, high_ref, three_ref, raw_ref,
        od_ref, ret_ref, acc_ref, side_ref, col_ref, pad_ref,
    )

    def collect(d, _):
        two_ref[d, :BLOCK] = ret_ref[CAP * d]
        two_ref[d, BLOCK : 2 * BLOCK] = ret_ref[CAP * d + 1]
        one_ref[d, :BLOCK] = ret_ref[CAP * d + 2]
        return 0

    lax.fori_loop(0, shards, collect, 0)
    parts = [row_ref[0], row_ref[1], col0_ref[...], col_ref[...]]
    parts = jnp.concatenate([x.astype(BF16) for x in parts], axis=0)
    two_ref[:, 2 * BLOCK :] = parts.reshape(shards, extra, BLOCK)
    one_ref[:, BLOCK:] = jnp.zeros((shards, extra, BLOCK), BF16)


def attend(
    head, slot_ref, edge_ref, qg_ref, kv_ref, low_ref, high_ref, far_ref, raw_ref,
    od_ref, ret_ref, acc_ref, side_ref, col_ref, pad_ref,
):
    blocks = qg_ref.shape[0]
    is_first, is_last = edge_ref[0], edge_ref[1]
    first = join(raw_ref[BLOCK : 2 * BLOCK], raw_ref[2 * BLOCK : 3 * BLOCK])[head]
    pad_ref[0] = join(low_ref[0], low_ref[1])[head]
    pad_ref[blocks + 1] = join(high_ref[0], high_ref[1])[head]
    pad_ref[1 : blocks + 1] = kv_ref[...]
    acc_ref[...] = jnp.zeros_like(acc_ref)
    ret_ref[...] = jnp.zeros_like(ret_ref)
    col_ref[...] = jnp.zeros_like(col_ref)

    def step(j, _):
        slot0, slot1 = slot_ref[2 * j], slot_ref[2 * j + 1]
        keep = 1.0 - ((j == 0) & (is_first == 1)).astype(F32)
        qg = qg_ref[j].astype(F32) * keep
        pair = query_pair(qg)
        window = pad_ref[pl.ds(j, 3)].reshape(3 * BLOCK, BLOCK)
        far0 = far_ref[slot0 // CAP, pl.ds(pl.multiple_of(slot0 % CAP * BLOCK, BLOCK), BLOCK)]
        far1 = far_ref[slot1 // CAP, pl.ds(pl.multiple_of(slot1 % CAP * BLOCK, BLOCK), BLOCK)]
        kv = jnp.concatenate([window, far0, far1, first], axis=0)
        both = dot(kv, pair, 1, 1)
        scores, gw = both[:, :BLOCK], both[:, BLOCK:]
        drop = (j == blocks - 1) & (is_last == 1)
        bias = jnp.where(drop, -jnp.inf, 0.0).astype(F32)
        scores = jnp.concatenate(
            [scores[: 2 * BLOCK], scores[2 * BLOCK : 3 * BLOCK] + bias, scores[3 * BLOCK :]], axis=0
        )
        peak = jnp.max(scores, axis=0, keepdims=True)
        expo = jnp.exp2((scores - peak) * LOG2E)
        weights = expo * (1.0 / jnp.sum(expo, axis=0, keepdims=True))
        wlow = weights.astype(BF16)
        kvt = kv.T
        out_t = dot(kvt, wlow, 1, 0)
        rounded = out_t.astype(BF16).astype(F32)
        row_dot = jnp.sum((rounded * qg.T)[HEAD_DIM:], axis=0, keepdims=True)
        ds = (weights * (gw - row_dot)).astype(BF16)
        dq_t = dot(kvt, ds, 1, 0)
        od_t = jnp.concatenate([dq_t[:HEAD_DIM] * SCALE, out_t[HEAD_DIM:]], axis=0)
        od_ref[j] = od_t.T.astype(BF16)
        terms = dot(jnp.concatenate([ds, wlow], axis=1), pair, 1, 0)
        acc_ref[pl.ds(j, 3)] += terms[: 3 * BLOCK].reshape(3, BLOCK, BLOCK)
        ret_ref[slot0] = terms[3 * BLOCK : 4 * BLOCK].astype(BF16)
        ret_ref[slot1] = terms[4 * BLOCK : 5 * BLOCK].astype(BF16)
        col_ref[...] += terms[5 * BLOCK :]
        return 0

    lax.fori_loop(0, blocks, step, 0)
    side_ref[0] = acc_ref[0].astype(BF16)
    side_ref[1] = acc_ref[blocks + 1].astype(BF16)


def raw_query(raw_ref):
    return join(raw_ref[:BLOCK], raw_ref[3 * BLOCK :])


def two_parts(x):
    high = x.astype(BF16)
    return high, (x - high.astype(F32)).astype(BF16)


def row_forward_kernel(raw_ref, kv0_ref, kv1_ref, stats_ref, peak_ref, out_ref, *, chunk):
    rows = []
    for h, kv_ref in enumerate((kv0_ref, kv1_ref)):
        qg = raw_query(raw_ref)[h].astype(F32)
        query = query_pair(qg)[:BLOCK]

        def step(c, carry, kv_ref=kv_ref, query=query):
            peak, total, out = carry
            kv = kv_ref[pl.ds(pl.multiple_of(c * chunk, chunk), chunk)]
            scores = dot(kv, query, 1, 1)
            new = jnp.maximum(peak, jnp.max(scores, axis=0, keepdims=True))
            shrink = jnp.exp2((peak - new) * LOG2E)
            expo = jnp.exp2((scores - new) * LOG2E)
            total = total * shrink + jnp.sum(expo, axis=0, keepdims=True)
            out = out * shrink + dot(kv, expo.astype(BF16), 0, 0)
            return new, total, out

        start = (
            jnp.full((1, BLOCK), -jnp.inf, F32),
            jnp.zeros((1, BLOCK), F32),
            jnp.zeros((BLOCK, BLOCK), F32),
        )
        peak, total, out = lax.fori_loop(0, kv_ref.shape[0] // chunk, step, start)
        point = peak.astype(BF16)
        shift = jnp.exp2((peak - point.astype(F32)) * LOG2E)
        out = out * shift
        row_dot = jnp.sum((out * qg.T)[HEAD_DIM:], axis=0, keepdims=True)
        rows += [point, *two_parts(total * shift), *two_parts(row_dot)]
        peak_ref[h : h + 1] = point.astype(F32)
        out_ref[h] = out
    rows = [r.astype(F32) for r in rows] + [jnp.zeros((6, BLOCK), F32)]
    stats_ref[...] = jnp.concatenate(rows, axis=0).astype(BF16)


def row_backward_kernel(
    raw_ref, kv0_ref, kv1_ref, all_ref, peak_ref, out_ref, far0_ref, far1_ref, row_ref, *, chunk
):
    stats = all_ref[...].astype(F32)
    for h, (kv_ref, far_ref) in enumerate(((kv0_ref, far0_ref), (kv1_ref, far1_ref))):
        qg = raw_query(raw_ref)[h].astype(F32)
        pair = query_pair(qg)
        row = [stats[:, 5 * h + i] for i in range(5)]
        peak = jnp.max(row[0], axis=0, keepdims=True)
        grow = jnp.exp2((row[0] - peak) * LOG2E)
        scale = 1.0 / jnp.sum((row[1] + row[2]) * grow, axis=0, keepdims=True)
        row_dot = jnp.sum((row[3] + row[4]) * grow, axis=0, keepdims=True) * scale

        def step(c, dq_t, kv_ref=kv_ref, far_ref=far_ref, pair=pair, peak=peak, scale=scale, row_dot=row_dot):
            rows = pl.ds(pl.multiple_of(c * chunk, chunk), chunk)
            kv = kv_ref[rows]
            both = dot(kv, pair, 1, 1)
            weights = jnp.exp2((both[:, :BLOCK] - peak) * LOG2E) * scale
            ds = (weights * (both[:, BLOCK:] - row_dot)).astype(BF16)
            far_ref[rows] = dot(jnp.concatenate([ds, weights.astype(BF16)], axis=1), pair, 1, 0)
            return dq_t + dot(kv, ds, 0, 0)

        dq_t = lax.fori_loop(0, kv_ref.shape[0] // chunk, step, jnp.zeros((BLOCK, BLOCK), F32))
        out_t = out_ref[h] * (jnp.exp2((peak_ref[h : h + 1] - peak) * LOG2E) * scale)
        row_ref[h] = jnp.concatenate([dq_t[:HEAD_DIM] * SCALE, out_t[HEAD_DIM:]], axis=0).T


def add_slots(tot_ref, wanted_ref, back_ref, ranks):
    def add(d, _):
        for at, r in enumerate(ranks):
            tot_ref[wanted_ref[CAP * d + r]] += back_ref[d, at * BLOCK : (at + 1) * BLOCK].astype(F32)
        return 0

    lax.fori_loop(0, back_ref.shape[0], add, 0)


def own_rows(h, tot_ref, acc_ref, far_ref, left_ref, right_ref):
    blocks = tot_ref.shape[0]
    tot_ref[...] = acc_ref[1 : blocks + 1] + far_ref[...].reshape(tot_ref.shape)
    tot_ref[blocks - 1] += right_ref[h].astype(F32)
    tot_ref[0] += left_ref[h].astype(F32)


def total0_kernel(
    wanted_ref, acc_ref, far_ref, left_ref, right_ref, three_ref, out_ref, block_ref, tot_ref
):
    own_rows(0, tot_ref, acc_ref, far_ref, left_ref, right_ref)
    add_slots(tot_ref, wanted_ref, three_ref, range(CAP))
    block_ref[...] = tot_ref[0]
    out_ref[...] = tot_ref[...].astype(BF16)


def total1_kernel(wanted_ref, acc_ref, far_ref, left_ref, right_ref, two_ref, tot_ref):
    own_rows(1, tot_ref, acc_ref, far_ref, left_ref, right_ref)
    add_slots(tot_ref, wanted_ref, two_ref, range(2))


def last_kernel(
    wanted_ref, edge_ref, part_ref, late_ref, head0_ref, block_ref, att_ref, dq_ref,
    dk_ref, dv_ref, att_out, dq_out, add_ref,
):
    step, count = pl.program_id(0), dk_ref.shape[0]
    keep = edge_ref[0].astype(F32)

    @pl.when(step == 0)
    def _():
        add_ref[...] = jnp.zeros_like(add_ref)

        def add(d, _):
            add_ref[wanted_ref[CAP * d + CAP - 1]] += late_ref[d, :BLOCK].astype(F32)
            return 0

        lax.fori_loop(0, late_ref.shape[0], add, 0)
        add_ref[0] += late_ref[:, BLOCK:].reshape(4 * BLOCK, BLOCK)[3 * BLOCK :].astype(F32) * keep

    for b in range(count):
        dk_ref[b], dv_ref[b] = join(head0_ref[b], part_ref[b] + add_ref[step * count + b])

    @pl.when(step == 0)
    def _():
        is_first = edge_ref[0] == 1
        root = late_ref[:, BLOCK:].reshape(4 * BLOCK, BLOCK).astype(F32)
        root = [root[i * BLOCK : (i + 1) * BLOCK] for i in range(4)]
        dk_ref[0], dv_ref[0] = join(
            block_ref[...] + root[2] * keep, part_ref[0] + add_ref[0]
        )
        for new, old_ref, out_ref in zip(join(root[0], root[1]), (dq_ref, att_ref), (dq_out, att_out)):
            out_ref[...] = jnp.where(is_first, new.astype(F32), old_ref[...].astype(F32)).astype(BF16)


def unpack_kernel(od0_ref, od1_ref, att_ref, dq_ref):
    def write(b, _):
        dq_ref[b], att_ref[b] = join(od0_ref[b], od1_ref[b])
        return 0

    lax.fori_loop(0, od0_ref.shape[0], write, 0)


def in_hbm(x):
    return pltpu.with_memory_space_constraint(x, pltpu.HBM)


def call(kernel, outs, operands, smem=0, scratch=(), us=2, loose=()):
    return pl.pallas_call(
        kernel,
        out_shape=[pltpu.HBM(s, d) for s, d in outs],
        in_specs=[in_smem] * smem + [in_vmem] * (len(operands) - smem),
        out_specs=[in_vmem] * len(outs),
        scratch_shapes=[pltpu.VMEM(s, d) for s, d in scratch],
        compiler_params=params(),
        cost_estimate=pl.CostEstimate(flops=us * 10**9, transcendentals=0, bytes_accessed=10**6),
    )(*(x if i < smem or i in loose else in_hbm(x) for i, x in enumerate(operands)))


def exchange(blocks):
    return lax.all_to_all(blocks, "seq", split_axis=0, concat_axis=0, tiled=True)


def after(x, done):
    return lax.optimization_barrier((x, done))


def per_device(query, key, value, grad_out, random_blocks):
    shards, here = lax.axis_size("seq"), lax.axis_index("seq")
    rows = query.shape[0]
    blocks = rows // BLOCK
    slots = shards * CAP
    extra = 4 * BLOCK // shards
    tile = (BLOCK, BLOCK)
    grid = (blocks, *tile)
    forward = [(i, i + 1) for i in range(shards - 1)]
    backward = [(i + 1, i) for i in range(shards - 1)]

    named = random_blocks.reshape(-1)
    owners, inner = named // blocks, named % blocks
    places = jnp.arange(named.shape[0])
    same = (owners[:, None] == owners[None, :]) & (places[None, :] < places[:, None])
    slot_of = owners * CAP + jnp.sum(same.astype(jnp.int32), axis=1)
    asked = jnp.sum(
        jnp.where(slot_of[None, :] == jnp.arange(slots)[:, None], inner[None, :], 0), axis=1
    ).reshape(shards, 1, CAP)
    asked = jnp.pad(asked.astype(BF16), ((0, 0), (0, 7), (0, BLOCK - CAP)))
    top = pl.BlockSpec(tile, lambda i: (0, 0))
    end = pl.BlockSpec(tile, lambda i: (blocks - 1, 0))
    query, key, value, grad_out = (in_hbm(x) for x in (query, key, value, grad_out))
    message, up, down = pl.pallas_call(
        ask_kernel,
        grid=(1,),
        out_shape=[
            pltpu.HBM((shards, extra + 8, BLOCK), BF16),
            pltpu.HBM((2, *tile), BF16),
            pltpu.HBM((2, *tile), BF16),
        ],
        in_specs=[pl.BlockSpec(asked.shape, lambda i: (0, 0, 0)), top, top, top, top, end, end],
        out_specs=[
            pl.BlockSpec((shards, extra + 8, BLOCK), lambda i: (0, 0, 0)),
            pl.BlockSpec((2, *tile), lambda i: (0, 0, 0)),
            pl.BlockSpec((2, *tile), lambda i: (0, 0, 0)),
        ],
        compiler_params=params(),
    )(asked, query, key, value, grad_out, key, value)
    got = exchange(message)
    wanted = got[:, extra, :CAP].astype(jnp.int32).reshape(-1)
    edge = jnp.stack([here == 0, here == shards - 1]).astype(jnp.int32)

    chunk = 512
    part = pl.BlockSpec((chunk, BLOCK), lambda i: (i, 0))

    def pack(a, b):
        return pl.pallas_call(
            pack_kernel,
            grid=(rows // chunk,),
            out_shape=[pltpu.HBM((rows, BLOCK), BF16)] * 2,
            in_specs=[part] * 2,
            out_specs=[part] * 2,
            compiler_params=params(),
        )(a, b)

    kv0, kv1 = pack(key, value)
    steps = 4
    (one0,) = call(
        gather0_kernel,
        [((shards, BLOCK + extra, BLOCK), BF16)],
        (wanted, kv0.reshape(grid), got[0, :extra]),
        smem=1,
        loose=(2,),
    )
    (two0,) = call(
        gather0_rest_kernel,
        [((shards, 2 * BLOCK, BLOCK), BF16)],
        (wanted, kv0.reshape(grid)),
        smem=1,
    )
    one0 = exchange(one0)
    query, grad_out, up, down, two0 = lax.optimization_barrier((query, grad_out, up, down, two0))
    qg0, qg1 = pack(in_hbm(query), in_hbm(grad_out))
    low = lax.ppermute(up, "seq", forward)
    high = lax.ppermute(down, "seq", backward)
    two0, one0, low, high = lax.optimization_barrier((two0, one0, low, high))
    two0 = exchange(two0)
    first = one0[:, BLOCK:].reshape(4 * BLOCK, BLOCK)
    stats, peak, partial = call(
        functools.partial(row_forward_kernel, chunk=chunk),
        [((16, BLOCK), BF16), ((2, BLOCK), F32), ((2, *tile), F32)],
        (first, kv0, kv1),
        us=8,
        loose=(0,),
    )
    (three1,) = call(
        gather1_kernel,
        [((shards, CAP * BLOCK + extra, BLOCK), BF16)],
        (wanted, kv1.reshape(grid), stats),
        smem=1,
        loose=(2,),
    )
    three1, two0 = after(three1, two0)
    three1 = exchange(three1)
    padded = ((blocks + 2, *tile), BF16)
    returns = ((slots, *tile), BF16)
    od0, back0, acc0, side0, col0 = call(
        main0_kernel,
        [
            (grid, BF16),
            ((shards, CAP * BLOCK, BLOCK), BF16),
            ((blocks + 2, *tile), F32),
            ((2, *tile), BF16),
            (tile, F32),
        ],
        (slot_of, edge, qg0.reshape(grid), kv0.reshape(grid), low, high, one0, two0, first),
        smem=2,
        loose=(4, 5, 6, 7, 8),
        scratch=[padded, ((shards, CAP * BLOCK, BLOCK), BF16), returns],
        us=38,
    )
    back0, three1 = after(back0, three1)
    back0 = exchange(back0)
    far0, far1, row_od = call(
        functools.partial(row_backward_kernel, chunk=chunk),
        [((rows, BLOCK), F32)] * 2 + [((2, *tile), F32)],
        (first, kv0, kv1, three1[:, CAP * BLOCK :], peak, partial),
        us=8,
        loose=(0, 3),
    )
    od1, two1, one1, acc1, side1 = call(
        main1_kernel,
        [
            (grid, BF16),
            ((shards, 2 * BLOCK + extra, BLOCK), BF16),
            ((shards, BLOCK + extra, BLOCK), BF16),
            ((blocks + 2, *tile), F32),
            ((2, *tile), BF16),
        ],
        (
            slot_of, edge, qg1.reshape(grid), kv1.reshape(grid), low, high, three1, first,
            row_od, col0,
        ),
        smem=2,
        loose=(4, 5, 6, 7),
        scratch=[padded, returns, (tile, F32)],
        us=38,
    )
    left = lax.ppermute(jnp.stack([side0[1], side1[1]]), "seq", forward)
    right = lax.ppermute(jnp.stack([side0[0], side1[0]]), "seq", backward)
    two1, back0, left, right = lax.optimization_barrier((two1, back0, left, right))
    two1 = exchange(two1)
    total = jnp.sum(two1[:, 2 * BLOCK :].astype(F32), axis=0).astype(BF16)
    one1 = one1.at[:, BLOCK:].set(jnp.broadcast_to(total, (shards, extra, BLOCK)))
    one1 = exchange(one1)
    attended, grad_query = call(unpack_kernel, [(grid, BF16)] * 2, (od0, od1), us=4)
    whole = [(grid, F32)]
    head0, block0 = call(
        total0_kernel,
        [(grid, BF16), (tile, F32)],
        (wanted, acc0, far0, left, right, back0),
        smem=1,
        scratch=whole,
        us=6,
        loose=(3, 4, 5),
    )
    (part1,) = call(
        total1_kernel,
        whole,
        (wanted, acc1, far1, left, right, two1),
        smem=1,
        us=4,
        loose=(3, 4, 5),
    )
    full = lambda shape: pl.BlockSpec(shape, lambda i: (0,) * len(shape))
    out_block = pl.BlockSpec((blocks // steps, *tile), lambda i: (i, 0, 0))
    attended, grad_query = (in_hbm(x.reshape(rows, BLOCK)) for x in (attended, grad_query))
    grad_key, grad_value, attended, grad_query = pl.pallas_call(
        last_kernel,
        grid=(steps,),
        out_shape=[pltpu.HBM(grid, BF16)] * 2 + [pltpu.HBM((rows, BLOCK), BF16)] * 2,
        in_specs=[in_smem, in_smem, out_block, full(one1.shape), out_block, full(tile), top, top],
        out_specs=[out_block, out_block, top, top],
        input_output_aliases={6: 2, 7: 3},
        scratch_shapes=[pltpu.VMEM(grid, F32)],
        compiler_params=params(),
        cost_estimate=pl.CostEstimate(flops=4 * 10**9, transcendentals=0, bytes_accessed=10**6),
    )(wanted, edge, in_hbm(part1), one1, in_hbm(head0), in_hbm(block0), attended, grad_query)
    return attended, grad_query, grad_key.reshape(rows, BLOCK), grad_value.reshape(rows, BLOCK)


def solution(mesh):
    split = P("seq", "head")
    return jax.shard_map(
        per_device,
        mesh=mesh,
        in_specs=(split, split, split, split, P("seq", None)),
        out_specs=(split, split, split, split),
        check_vma=False,
    )
```
